32 devices in a mesh: group: 2 (over y), line: 16 (over z, x, core).
Axes of the slice: x: 2, y: 2, z: 4, core: 2. Of those that a mesh axis runs over, the one named last changes fastest.
Arguments:
- residual_in: bfloat16 [2048, 2048], P(('group', 'line')), parts along dimension 0, may hold values from -6 to 6
- queries: bfloat16 [2048, 2048], P(('group', 'line')), parts along dimension 0, may hold values from -8 to 8
- question_key_values: bfloat16 [2048, 512], P(('group', 'line')), parts along dimension 0, may hold values from -8 to 8
- document_prefix_cache: bfloat16 [4096, 512], P(('group', 'line')), parts along dimension 0, may hold values from -8 to 8
- out_proj: bfloat16 [2048, 2048], P('line'), may hold values from -0.125 to 0.125
- norm_gain: float32 [2048], replicated, may hold values from 0.5 to 1.5
- routes: int32 [2048, 8], P(('group', 'line')), parts along dimension 0, may hold values from 0 to 15, all different within a row; in each aligned block of 32 rows (0 to 31, 32 to 63, ...) at most 32 rows name the same one
- keep_mask: int32 [2048, 8], P(('group', 'line')), parts along dimension 0, may hold values 0 or 1
- route_weights: float32 [2048, 8], P(('group', 'line')), parts along dimension 0, may hold values from 0.02 to 0.4
- expert_slots: int32 [16], replicated, may hold values from 0 to 15, each once
- expert_gate: bfloat16 [16, 2048, 768], P('line'), may hold values from -0.125 to 0.125
- expert_up: bfloat16 [16, 2048, 768], P('line'), may hold values from -0.125 to 0.125
- expert_down: bfloat16 [16, 768, 2048], P('line'), may hold values from -0.21875 to 0.21875
Outputs:
- layer_out: bfloat16 [2048, 2048], P(('group', 'line')), parts along dimension 0
The draws below stay inside these ranges and needn't reach their ends.
There are 2 independent parts, one for each index of `group`. The reference program is written for one: setup_inputs(seed, part) draws one part's arguments, and reference() takes and returns one part's arrays. A program takes and returns all parts, laid end to end along the dimension named above; an argument that names none is the same for every part. Nothing has to cross between parts.
Inputs may be any that keep to these rules, and one draw needn't show every extreme that they name: `routes`: each row names 8 different experts; in every aligned block of half of 64 rows no expert is named by more than 32 rows. `expert_slots`: every slot holds exactly one expert.
All inputs are finite; a program needn't handle non-finite values. No bound on the sum of `keep_mask` on one device may be relied on, other than what follows from the above.
Results may differ from the reference program's by a relative error of at most 0.0045.
Values may be sent and summed in bfloat16 or wider, within the bound.
No kernel may reach another device: no remote copies, remote signals or barrier semaphores. Data moves between devices by JAX's collectives and lax.ppermute only.
A program may use at most 256 MiB of HBM per device.

```python
import math
import jax
import jax.numpy as jnp
import numpy as np
from jax import lax

D = 2048
QUERY_HEADS = 16
KEY_VALUE_HEADS = 2
HEAD_SIZE = 128
FF = 768
TOPK = 8
QLEN = 16
TOKENS_PER_LINE = 64
TOKEN_TOTAL = 1024
PREFIX_LENGTH = 2048
EXPERTS = 16
HCAP = 32


def draw_document_prefix_cache(key, part):
    key_portion, value_portion = jax.random.split(jax.random.fold_in(key, 5))
    key_matrix = jnp.clip(jax.random.normal(key_portion, (PREFIX_LENGTH, KEY_VALUE_HEADS, HEAD_SIZE), jnp.float32), -6.0, 6.0)
    value_matrix = jnp.clip(jax.random.normal(value_portion, (PREFIX_LENGTH, KEY_VALUE_HEADS, HEAD_SIZE), jnp.float32), -6.0, 6.0)
    return jnp.concatenate([key_matrix.reshape(PREFIX_LENGTH, KEY_VALUE_HEADS * HEAD_SIZE), value_matrix.reshape(PREFIX_LENGTH, KEY_VALUE_HEADS * HEAD_SIZE)], axis=1).astype(jnp.bfloat16)


def draw_queries(key, part):
    base_key = jax.random.fold_in(key, 9)
    query_table = jnp.clip(2.0 * jax.random.normal(base_key, (TOKEN_TOTAL, QUERY_HEADS * HEAD_SIZE), jnp.float32), -8.0, 8.0)
    return query_table.astype(jnp.bfloat16)


def draw_question_key_values(key, part):
    key_portion, value_portion = jax.random.split(jax.random.fold_in(key, 13))
    key_matrix = jnp.clip(1.6 * jax.random.normal(key_portion, (TOKEN_TOTAL, KEY_VALUE_HEADS * HEAD_SIZE), jnp.float32), -8.0, 8.0)
    value_matrix = jnp.clip(jax.random.normal(value_portion, (TOKEN_TOTAL, KEY_VALUE_HEADS * HEAD_SIZE), jnp.float32), -6.0, 6.0)
    return jnp.concatenate([key_matrix, value_matrix], axis=1).astype(jnp.bfloat16)


def touch_ends(values, stream_key, smallest, largest):
    shape = values.shape
    place = [jax.random.randint(jax.random.fold_in(stream_key, axis), (), 0, shape[axis]) for axis in range(len(shape))]
    values = values.at[tuple(place)].set(smallest)
    longest = shape.index(max(shape))
    place[longest] = (place[longest] + 1) % shape[longest]
    return values.at[tuple(place)].set(largest)


def shard_levels(own_key, shape, cuts, smallest, high):
    level, own = 1.0, jax.random.fold_in(own_key, 6)
    for dim, blocks in cuts:
        steps = jnp.exp(jax.random.uniform(jax.random.fold_in(own, dim), (blocks,), jnp.float32, smallest / len(cuts), high / len(cuts)))
        level = level * jnp.repeat(steps, shape[dim] // blocks).reshape([-1 if axis == dim else 1 for axis in range(len(shape))])
    return level


def shared_out(key, own, number, rows, amount, top, bound, skew):
    sequence = jax.random.permutation(key, amount)
    packed, common = shares(amount, rows * top, bound, skew, True), shares(amount, rows * top, bound, skew, False)
    places = jnp.arange(amount)

    def named(tallies, turn):
        used = int((tallies > 0).sum())
        fixed = max(1, used // 4)
        passed = fixed + (places - fixed + turn * (used - fixed)) % max(1, amount - fixed)
        return jnp.zeros((amount,), jnp.int32).at[sequence[jnp.where(places < fixed, places, passed)]].set(jnp.asarray(tallies, jnp.int32))

    tallies = jnp.where(number % 4 == 0, named(packed, number // 4), named(common, number - number // 4 - 1))
    mixed = jax.random.permutation(jax.random.fold_in(own, 3), amount)
    donor, sink = mixed[0:amount // 2 * 2:2], mixed[1:amount // 2 * 2:2]
    margin = jnp.minimum(tallies[donor] - 1, bound - tallies[sink]) // 2
    margin = jnp.where((donor == sequence[0]) | (sink == sequence[0]) | (tallies[sink] == 0), 0, jnp.maximum(margin, 0))
    passed = jax.random.randint(jax.random.fold_in(own, 4), (amount // 2,), 0, 1 << 20) % (margin + 1)
    tallies = tallies.at[donor].add(-passed).at[sink].add(passed)
    items = jnp.searchsorted(jnp.cumsum(tallies), jnp.arange(rows * top), side="right").astype(jnp.int32)
    listing = items.reshape(top, rows).T
    listing = listing[jax.random.permutation(jax.random.fold_in(own, 1), rows)]
    turn = jax.random.randint(jax.random.fold_in(own, 2), (rows, 1), 0, top)
    return jnp.take_along_axis(listing, (jnp.arange(top)[None, :] + turn) % top, axis=1)


def shares(number_of, total, bound, slope, full):
    portions = [(1 << 20) // math.isqrt(grade ** slope) + 1 for grade in range(1, number_of + 1)]
    largest = bound if full else min(bound, max(-(-total // number_of), total * portions[0] // sum(portions)))
    least = 1 if total - largest >= number_of - 1 else 0
    given, surplus = [largest] + [least] * (number_of - 1), total - largest - least * (number_of - 1)
    while surplus > 0:
        free = [i for i in range(1, number_of) if given[i] < largest] or [i for i in range(1, number_of) if given[i] < bound]
        mass, budget = sum([portions[i] for i in free]), surplus
        for i in free:
            addition = min(bound - given[i], max(1, budget * portions[i] // mass), surplus)
            given[i] = given[i] + addition
            surplus = surplus - addition
    return np.array(given)


def normal_values(key, dims, width, most, pieces=(), kind=jnp.bfloat16):
    result = jax.random.normal(key, dims, jnp.float32) * width
    if len(pieces) > 0:
        result = shard_levels(key, dims, pieces, -0.22, 0.18) * result
    return jnp.clip(result, min=-most, max=most).astype(kind)


def setup_inputs(seed: int = 0, part: int = 0) -> dict:
    seeds = jax.random.split(jax.random.key(seed), 14)
    part_keys = jax.random.split(jax.random.fold_in(seeds[13], part), 14)
    residual_in = normal_values(part_keys[0], (TOKEN_TOTAL, D), 1.0, 6.0, ((0, 16),))
    queries = draw_queries(jax.random.fold_in(jax.random.fold_in(seeds[13], part), 71), part)
    question_key_values = draw_question_key_values(jax.random.fold_in(jax.random.fold_in(seeds[13], part), 71), part)
    document_prefix_cache = draw_document_prefix_cache(jax.random.fold_in(jax.random.fold_in(seeds[13], part), 71), part)
    out_proj = normal_values(seeds[4], (QUERY_HEADS * HEAD_SIZE, D), (QUERY_HEADS * HEAD_SIZE) ** -0.5, 0.125, ((0, 16),))
    norm_gain = jnp.clip(1.0 + 0.1 * jax.random.normal(seeds[5], (D,), jnp.float32), 0.5, 1.5)
    routes_keys = jax.random.split(jax.random.fold_in(part_keys[6], 1), TOKEN_TOTAL // (TOKENS_PER_LINE // 2))
    routes_turns = jax.random.permutation(jax.random.fold_in(part_keys[6], 3), TOKEN_TOTAL // (TOKENS_PER_LINE // 2))
    routes = jax.vmap(lambda own, number: shared_out(jax.random.fold_in(part_keys[6], 2), own, number, TOKENS_PER_LINE // 2, EXPERTS, TOPK, HCAP, 2))(routes_keys, routes_turns).reshape((TOKEN_TOTAL, TOPK))
    keep_mask = touch_ends((jax.random.randint(part_keys[7], (TOKEN_TOTAL, TOPK), 0, 4) < 3).astype(jnp.int32), jax.random.fold_in(part_keys[7], 1), 0, 1)
    route_weights = jnp.clip(jnp.exp(math.log(0.4) - 2.9957323 * jax.random.uniform(part_keys[8], (TOKEN_TOTAL, TOPK), jnp.float32) ** shard_levels(part_keys[8], (TOKEN_TOTAL, TOPK), ((0, 16),), -0.2, 0.2)), 0.02, 0.4)
    expert_slots = jax.random.permutation(seeds[9], EXPERTS).astype(jnp.int32)
    expert_gate = normal_values(seeds[10], (EXPERTS, D, FF), D ** -0.5, 0.125, ((0, 16),))
    expert_up = normal_values(seeds[11], (EXPERTS, D, FF), D ** -0.5, 0.125, ((0, 16),))
    expert_down = normal_values(seeds[12], (EXPERTS, FF, D), FF ** -0.5, 0.21875, ((0, 16),))
    return {"residual_in": residual_in, "queries": queries, "question_key_values": question_key_values, "document_prefix_cache": document_prefix_cache, "out_proj": out_proj, "norm_gain": norm_gain, "routes": routes, "keep_mask": keep_mask, "route_weights": route_weights, "expert_slots": expert_slots, "expert_gate": expert_gate, "expert_up": expert_up, "expert_down": expert_down}


def block_attention(paired_blocks, document_keys, document_values, visible_mask):
    queries_per_key_head = QUERY_HEADS // KEY_VALUE_HEADS
    score_scale = 1.0 / math.sqrt(HEAD_SIZE)
    block_of_queries, local_block = paired_blocks
    heads_of_queries = block_of_queries.reshape(TOKENS_PER_LINE, KEY_VALUE_HEADS, queries_per_key_head, HEAD_SIZE).astype(jnp.float32)
    local_keys = local_block[:, :KEY_VALUE_HEADS * HEAD_SIZE].reshape(TOKENS_PER_LINE, KEY_VALUE_HEADS, HEAD_SIZE).astype(jnp.float32)
    local_values = local_block[:, KEY_VALUE_HEADS * HEAD_SIZE:].reshape(TOKENS_PER_LINE, KEY_VALUE_HEADS, HEAD_SIZE).astype(jnp.float32)
    far_scores = jnp.einsum('thgd,nhd->thgn', heads_of_queries, document_keys) * score_scale
    near_scores = jnp.einsum('thgd,shd->thgs', heads_of_queries, local_keys) * score_scale
    near_scores = jnp.where(visible_mask[:, None, None, :], near_scores, -1e+30)
    row_max = jnp.maximum(far_scores.max(-1), near_scores.max(-1))
    far_terms = jnp.exp(far_scores - row_max[..., None])
    near_terms = jnp.exp(near_scores - row_max[..., None])
    denominator = far_terms.sum(-1) + near_terms.sum(-1)
    far_probs = lax.optimization_barrier(far_terms.astype(jnp.bfloat16)).astype(jnp.float32)
    near_probs = lax.optimization_barrier(near_terms.astype(jnp.bfloat16)).astype(jnp.float32)
    summed = jnp.einsum('thgn,nhd->thgd', far_probs, document_values) + jnp.einsum('thgs,shd->thgd', near_probs, local_values)
    return (summed / denominator[..., None]).reshape(TOKENS_PER_LINE, QUERY_HEADS * HEAD_SIZE).astype(jnp.bfloat16)

def reference(residual_in, queries, question_key_values, document_prefix_cache, out_proj, norm_gain, routes, keep_mask, route_weights, expert_slots, expert_gate, expert_up, expert_down):
    document_keys = document_prefix_cache[:, :KEY_VALUE_HEADS * HEAD_SIZE].reshape(PREFIX_LENGTH, KEY_VALUE_HEADS, HEAD_SIZE).astype(jnp.float32)
    document_values = document_prefix_cache[:, KEY_VALUE_HEADS * HEAD_SIZE:].reshape(PREFIX_LENGTH, KEY_VALUE_HEADS, HEAD_SIZE).astype(jnp.float32)
    position = jnp.arange(TOKENS_PER_LINE, dtype=jnp.int32)
    visible_mask = (position[:, None] // QLEN == position[None, :] // QLEN) & (position[None, :] <= position[:, None])
    block_list = TOKEN_TOTAL // TOKENS_PER_LINE
    context_rows = lax.map(lambda paired_blocks: block_attention(paired_blocks, document_keys, document_values, visible_mask), (queries.reshape(block_list, TOKENS_PER_LINE, QUERY_HEADS * HEAD_SIZE), question_key_values.reshape(block_list, TOKENS_PER_LINE, 2 * KEY_VALUE_HEADS * HEAD_SIZE)))
    context_rows = context_rows.reshape(TOKEN_TOTAL, QUERY_HEADS * HEAD_SIZE)
    mixture = residual_in.astype(jnp.float32) + jnp.dot(context_rows, out_proj, preferred_element_type=jnp.float32)
    normed = (mixture * lax.rsqrt(lax.optimization_barrier(jnp.mean(mixture * mixture, axis=-1, keepdims=True)) + 1e-06) * norm_gain).astype(jnp.bfloat16)
    flat_experts = jnp.where(keep_mask.reshape(-1) > 0, routes.reshape(-1), EXPERTS).astype(jnp.int32)
    order = jnp.argsort(flat_experts, stable=True).astype(jnp.int32)
    numbers = jnp.arange(EXPERTS, dtype=jnp.int32)
    counts = lax.optimization_barrier(jnp.sum((flat_experts[:, None] == numbers[None, :]).astype(jnp.int32), axis=0)).astype(jnp.int32)
    starts = (jnp.cumsum(counts) - counts).astype(jnp.int32)
    block_rows = 128
    order_padded = jnp.concatenate([order, jnp.zeros((block_rows,), jnp.int32)])
    weights_flat = route_weights.reshape(-1)
    lane_index = jnp.arange(block_rows, dtype=jnp.int32)

    def expert_step(expert, expert_total):
        slot_number = expert_slots[expert]
        gate_weights = lax.dynamic_index_in_dim(expert_gate, slot_number, 0, keepdims=False)
        up_weights = lax.dynamic_index_in_dim(expert_up, slot_number, 0, keepdims=False)
        down_weights = lax.dynamic_index_in_dim(expert_down, slot_number, 0, keepdims=False)
        load_count = counts[expert]
        load_start = starts[expert]

        def unfinished(loop_state):
            return loop_state[0] * block_rows < load_count

        def run_block(loop_state):
            block_number, running = loop_state
            pair_index = lax.dynamic_slice_in_dim(order_padded, load_start + block_number * block_rows, block_rows)
            valid = lane_index < load_count - block_number * block_rows
            token_index = (pair_index // TOPK).astype(jnp.int32)
            picked_rows = normed[token_index]
            gate_proj = jnp.dot(picked_rows, gate_weights, preferred_element_type=jnp.float32)
            upper = jnp.dot(picked_rows, up_weights, preferred_element_type=jnp.float32)
            middle = (jax.nn.silu(gate_proj) * upper).astype(jnp.bfloat16)
            answer = jnp.dot(middle, down_weights, preferred_element_type=jnp.float32).astype(jnp.bfloat16)
            answer = lax.optimization_barrier(answer).astype(jnp.float32)
            scaled = answer * jnp.where(valid, weights_flat[pair_index], 0.0)[:, None]
            return (block_number + 1, running.at[token_index].add(scaled))
        return lax.while_loop(unfinished, run_block, (jnp.int32(0), expert_total))[1]
    expert_sum = lax.fori_loop(0, EXPERTS, expert_step, jnp.zeros((TOKEN_TOTAL, D), jnp.float32))
    return (mixture + expert_sum).astype(jnp.bfloat16)
```

```python
import math

import jax
import jax.numpy as jnp
from jax import lax
from jax.sharding import PartitionSpec as P

QUERY_HEADS = 16
KEY_VALUE_HEADS = 2
HEAD_SIZE = 128
TOPK = 8
QLEN = 16


def partner(array, axis, bit):
    return lax.ppermute(array, axis, [(i, i ^ 1 << bit) for i in range(lax.axis_size(axis))])


def shifted(value, axis, steps):
    count = lax.axis_size(axis)
    pairs = [(source, (source + steps) % count) for source in range(count)]
    return lax.ppermute(value, axis, pairs)


def expert_answers(received, expert_gate, expert_up, expert_down):
    buffer_shape = received.shape
    flat_rows = received.reshape(-1, buffer_shape[-1])
    gate_proj = jnp.dot(flat_rows, expert_gate[0], preferred_element_type=jnp.float32)
    upper = jnp.dot(flat_rows, expert_up[0], preferred_element_type=jnp.float32)
    middle = (jax.nn.silu(gate_proj) * upper).astype(jnp.bfloat16)
    return (
        jnp.dot(middle, expert_down[0], preferred_element_type=jnp.float32)
        .astype(jnp.bfloat16)
        .reshape(buffer_shape)
    )


def mix_experts(
    normed_rows,
    route_rows,
    keep_rows,
    weight_rows,
    expert_slots,
    expert_gate,
    expert_up,
    expert_down,
    slot_cap,
):
    row_count = normed_rows.shape[0]
    model_width = normed_rows.shape[1]
    line_count = lax.axis_size("line")
    pair_count = row_count * TOPK
    expert_ids = route_rows.reshape(pair_count)
    kept_pairs = keep_rows.reshape(pair_count) > 0
    numbers = jnp.arange(expert_slots.shape[0], dtype=jnp.int32)
    matches = expert_ids[:, None] == numbers[None, :]
    target = jnp.sum(jnp.where(matches, expert_slots[None, :], 0), axis=1)
    chosen = (matches & kept_pairs[:, None]).astype(jnp.bfloat16)
    pair_order = jnp.arange(pair_count, dtype=jnp.int32)
    earlier = (pair_order[:, None] > pair_order[None, :]).astype(jnp.bfloat16)
    before = jnp.dot(earlier, chosen, preferred_element_type=jnp.float32)
    slot_rank = jnp.sum(before * chosen.astype(jnp.float32), axis=1).astype(jnp.int32)
    slot_index = jnp.where(kept_pairs, target * slot_cap + slot_rank, line_count * slot_cap)
    slot_owner = (
        jnp.full((line_count * slot_cap,), pair_count, jnp.int32)
        .at[slot_index]
        .set(pair_order, mode="drop")
    )
    source_row = jnp.where(slot_owner < pair_count, slot_owner // TOPK, row_count)
    padded = jnp.concatenate([normed_rows, jnp.zeros((1, model_width), jnp.bfloat16)], axis=0)
    buffer = padded[source_row].reshape(line_count, slot_cap, model_width)
    returned = lax.all_to_all(
        expert_answers(
            lax.all_to_all(buffer, "line", split_axis=0, concat_axis=0, tiled=True),
            expert_gate,
            expert_up,
            expert_down,
        ),
        "line",
        split_axis=0,
        concat_axis=0,
        tiled=True,
    )
    padded_back = jnp.concatenate(
        [
            returned.reshape(line_count * slot_cap, model_width),
            jnp.zeros((1, model_width), jnp.bfloat16),
        ],
        axis=0,
    )
    per_pair = padded_back[slot_index].reshape(row_count, TOPK, model_width)
    weight = jnp.where(kept_pairs, weight_rows.reshape(pair_count), 0.0).reshape(row_count, TOPK)
    return jnp.sum(per_pair.astype(jnp.float32) * weight[:, :, None], axis=1)


def near_state(heads_of_queries, local_keys, local_values, score_scale):
    local_tokens = heads_of_queries.shape[0]
    near_scores = (
        jnp.einsum(
            "thgd,shd->thgs", heads_of_queries, local_keys, preferred_element_type=jnp.float32
        )
        * score_scale
    )
    position = jnp.arange(local_tokens, dtype=jnp.int32)
    visible_mask = (position[:, None] // QLEN == position[None, :] // QLEN) & (
        position[None, :] <= position[:, None]
    )
    near_scores = jnp.where(visible_mask[:, None, None, :], near_scores, -1e30)
    run_max = near_scores.max(-1)
    exp_terms = jnp.exp(near_scores - run_max[..., None])
    run_sum = exp_terms.sum(-1)
    run_acc = jnp.einsum(
        "thgs,shd->thgd",
        exp_terms.astype(jnp.bfloat16),
        local_values,
        preferred_element_type=jnp.float32,
    )
    return (run_max, run_sum, run_acc)


def fold_block(carry, piece, heads_of_queries, kv_heads, score_scale):
    old_max, old_sum, old_acc = carry
    piece_rows = piece.shape[0]
    piece_keys = piece[:, : kv_heads * HEAD_SIZE].reshape(piece_rows, kv_heads, HEAD_SIZE)
    piece_vals = piece[:, kv_heads * HEAD_SIZE :].reshape(piece_rows, kv_heads, HEAD_SIZE)
    far_scores = (
        jnp.einsum(
            "thgd,nhd->thgn", heads_of_queries, piece_keys, preferred_element_type=jnp.float32
        )
        * score_scale
    )
    new_max = jnp.maximum(old_max, far_scores.max(-1))
    factor = jnp.exp(old_max - new_max)
    far_terms = jnp.exp(far_scores - new_max[..., None])
    new_acc = old_acc * factor[..., None] + jnp.einsum(
        "thgn,nhd->thgd",
        far_terms.astype(jnp.bfloat16),
        piece_vals,
        preferred_element_type=jnp.float32,
    )
    return (new_max, old_sum * factor + far_terms.sum(-1), new_acc)


def body(
    residual_in,
    queries,
    question_key_values,
    document_prefix_cache,
    out_proj,
    norm_gain,
    routes,
    keep_mask,
    route_weights,
    expert_slots,
    expert_gate,
    expert_up,
    expert_down,
):
    local_tokens = queries.shape[0]
    queries_per_key_head = QUERY_HEADS // KEY_VALUE_HEADS
    score_scale = 1.0 / math.sqrt(HEAD_SIZE)
    half_kv = KEY_VALUE_HEADS // 2
    query_width = half_kv * queries_per_key_head * HEAD_SIZE
    kv_width = half_kv * HEAD_SIZE
    member = lax.axis_index("line") % 2
    other = 1 - member
    query_split = queries.reshape(local_tokens, 2, query_width)
    key_split = question_key_values[:, : KEY_VALUE_HEADS * HEAD_SIZE].reshape(
        local_tokens, 2, kv_width
    )
    value_split = question_key_values[:, KEY_VALUE_HEADS * HEAD_SIZE :].reshape(
        local_tokens, 2, kv_width
    )
    own_pack = jnp.concatenate(
        [
            lax.dynamic_index_in_dim(query_split, member, 1, keepdims=False),
            lax.dynamic_index_in_dim(key_split, member, 1, keepdims=False),
            lax.dynamic_index_in_dim(value_split, member, 1, keepdims=False),
        ],
        axis=1,
    )
    send_pack = jnp.concatenate(
        [
            lax.dynamic_index_in_dim(query_split, other, 1, keepdims=False),
            lax.dynamic_index_in_dim(key_split, other, 1, keepdims=False),
            lax.dynamic_index_in_dim(value_split, other, 1, keepdims=False),
        ],
        axis=1,
    )
    partner_pack = partner(send_pack, "line", 0)
    both_pack = jnp.concatenate([own_pack, partner_pack], axis=0)
    pair_rows = both_pack.shape[0]
    heads_of_queries = both_pack[:, :query_width].reshape(
        pair_rows, half_kv, queries_per_key_head, HEAD_SIZE
    )
    local_keys = both_pack[:, query_width : query_width + kv_width].reshape(
        pair_rows, half_kv, HEAD_SIZE
    )
    local_values = both_pack[:, query_width + kv_width :].reshape(pair_rows, half_kv, HEAD_SIZE)
    start_state = near_state(heads_of_queries, local_keys, local_values, score_scale)
    prefix_rows = document_prefix_cache.shape[0]
    document_keys = document_prefix_cache[:, : KEY_VALUE_HEADS * HEAD_SIZE].reshape(
        prefix_rows, 2, kv_width
    )
    document_values = document_prefix_cache[:, KEY_VALUE_HEADS * HEAD_SIZE :].reshape(
        prefix_rows, 2, kv_width
    )
    own_slab = jnp.concatenate(
        [
            lax.dynamic_index_in_dim(document_keys, member, 1, keepdims=False),
            lax.dynamic_index_in_dim(document_values, member, 1, keepdims=False),
        ],
        axis=1,
    )
    send_slab = jnp.concatenate(
        [
            lax.dynamic_index_in_dim(document_keys, other, 1, keepdims=False),
            lax.dynamic_index_in_dim(document_values, other, 1, keepdims=False),
        ],
        axis=1,
    )
    slab = jnp.concatenate([own_slab, partner(send_slab, "line", 0)], axis=0)
    levels = (lax.axis_size("line") // 2).bit_length() - 1
    for level in range(levels):
        slab = jnp.concatenate([slab, shifted(slab, "line", 2 * (1 << level))], axis=0)
    slab_rows = slab.shape[0]
    block_rows = math.gcd(slab_rows, 2048)
    slab_blocks = slab.reshape(slab_rows // block_rows, block_rows, 2 * kv_width)

    def scan_step(carry, piece):
        return (fold_block(carry, piece, heads_of_queries, half_kv, score_scale), None)

    final_state, unused = lax.scan(scan_step, start_state, slab_blocks)
    run_max, run_sum, run_acc = final_state
    pair_context = (
        (run_acc / run_sum[..., None]).reshape(pair_rows, query_width).astype(jnp.bfloat16)
    )
    mine = pair_context[:local_tokens]
    returned_context = partner(pair_context[local_tokens:], "line", 0)
    context_rows = jnp.where(
        member == 0,
        jnp.concatenate([mine, returned_context], axis=1),
        jnp.concatenate([returned_context, mine], axis=1),
    )
    attended = jnp.dot(
        context_rows,
        lax.all_gather(out_proj, "line", axis=0, tiled=True),
        preferred_element_type=jnp.float32,
    )
    mixture = residual_in.astype(jnp.float32) + attended
    normed = (
        mixture * lax.rsqrt(jnp.mean(mixture * mixture, axis=-1, keepdims=True) + 1e-06) * norm_gain
    ).astype(jnp.bfloat16)
    half_cap = local_tokens * TOPK // expert_slots.shape[0]
    expert_sum = mix_experts(
        normed,
        routes,
        keep_mask,
        route_weights,
        expert_slots,
        expert_gate,
        expert_up,
        expert_down,
        2 * half_cap,
    )
    return (mixture + expert_sum).astype(jnp.bfloat16)


def ring_spot(pair, pairs):
    row, column = divmod(pair, 2)
    return row if column == 0 else pairs - 1 - row


def ring_pair(spot, pairs):
    return 2 * spot if spot < pairs // 2 else 2 * (pairs - 1 - spot) + 1


def around(value, steps):
    count = lax.axis_size("line")
    pairs = count // 2
    moves = [
        (i, 2 * ring_pair((ring_spot(i // 2, pairs) + steps) % pairs, pairs) + i % 2)
        for i in range(count)
    ]
    return lax.ppermute(value, "line", moves)


def ring_gather(value):
    pairs = lax.axis_size("line") // 2
    found = {0: value}
    for step in range(1, pairs // 2 + 1):
        found[-step] = around(found[1 - step], 1)
        if step < pairs - pairs // 2:
            found[step] = around(found[step - 1], -1)
    return found


def ring_sum(parts):
    ahead = max(parts) + 1
    behind = min(parts)
    pairs = len(parts)
    forward = parts[behind].astype(jnp.bfloat16)
    backward = parts[behind + 1].astype(jnp.bfloat16)
    for step in range(1, -behind + 1):
        forward = around(forward, 1)
        if step < -behind:
            forward = (parts[-behind - step] + forward.astype(jnp.float32)).astype(jnp.bfloat16)
        if step < ahead:
            backward = around(backward, -1)
            if step < ahead - 1:
                backward = (parts[step - ahead + 1] + backward.astype(jnp.float32)).astype(
                    jnp.bfloat16
                )
    return parts[0] + forward.astype(jnp.float32) + backward.astype(jnp.float32)


def slot_weights(route_rows, keep_rows, weight_rows, expert_slots):
    numbers = jnp.arange(expert_slots.shape[0], dtype=jnp.int32)
    target = jnp.sum(
        jnp.where(route_rows[:, :, None] == numbers, expert_slots[None, None, :], 0), axis=2
    )
    kept = jnp.where(keep_rows > 0, weight_rows, 0.0)
    return jnp.sum(jnp.where(target[:, :, None] == numbers, kept[:, :, None], 0.0), axis=1)


def three_parts(values):
    high = lax.reduce_precision(values, 8, 7)
    rest = values - high
    middle = lax.reduce_precision(rest, 8, 7)
    return [part.astype(jnp.bfloat16) for part in (high, middle, rest - middle)]


def one_expert(rows, gate, up, down):
    gate_proj = jnp.dot(rows, gate, preferred_element_type=jnp.float32)
    upper = jnp.dot(rows, up, preferred_element_type=jnp.float32)
    middle = (jax.nn.silu(gate_proj) * upper).astype(jnp.bfloat16)
    return jnp.dot(middle, down, preferred_element_type=jnp.float32).astype(jnp.bfloat16)


def two_experts(rows, weights, experts):
    return sum(
        one_expert(rows, *expert).astype(jnp.float32) * weights[:, number : number + 1]
        for number, expert in enumerate(experts)
    )


def ring_body(
    residual_in,
    queries,
    question_key_values,
    document_prefix_cache,
    out_proj,
    norm_gain,
    routes,
    keep_mask,
    route_weights,
    expert_slots,
    expert_gate,
    expert_up,
    expert_down,
):
    local_tokens = queries.shape[0]
    heads_per_kv = QUERY_HEADS // KEY_VALUE_HEADS
    score_scale = 1.0 / math.sqrt(HEAD_SIZE)
    query_width = heads_per_kv * HEAD_SIZE
    line = lax.axis_index("line")
    pairs = lax.axis_size("line") // 2
    member = line % 2
    other = 1 - member
    pair_at = jnp.array([ring_pair(spot, pairs) for spot in range(pairs)], jnp.int32)
    spot_at = jnp.array([ring_spot(pair, pairs) for pair in range(pairs)], jnp.int32)
    spot = spot_at[line // 2]

    def half(array, which):
        return lax.dynamic_slice_in_dim(
            array, which * (array.shape[1] // 2), array.shape[1] // 2, axis=1
        )

    def both(left, right, which):
        return jnp.concatenate([half(left, which), half(right, which)], axis=1)

    kv_columns = KEY_VALUE_HEADS * HEAD_SIZE
    prefix_keys = document_prefix_cache[:, :kv_columns]
    prefix_values = document_prefix_cache[:, kv_columns:]
    slab = jnp.concatenate(
        [
            both(prefix_keys, prefix_values, member),
            partner(both(prefix_keys, prefix_values, other), "line", 0),
        ],
        axis=0,
    )
    slots = expert_slots.shape[0]
    pieces = three_parts(slot_weights(routes, keep_mask, route_weights, expert_slots))
    weight_lanes = -(-3 * slots // 64) * 64
    pieces.append(jnp.zeros((local_tokens, weight_lanes - 3 * slots), jnp.bfloat16))
    weight_rows = jnp.concatenate(pieces, axis=1).reshape(-1, 2 * HEAD_SIZE)
    arrived = ring_gather(jnp.concatenate([slab, weight_rows], axis=0))
    offsets = sorted(arrived)
    prefix = jnp.concatenate([arrived[o][: slab.shape[0]] for o in offsets], axis=0)
    all_weights = jnp.concatenate([arrived[o][slab.shape[0] :] for o in offsets], axis=0).reshape(
        -1, weight_lanes
    )
    lane = jnp.arange(weight_lanes, dtype=jnp.int32)
    wanted = jnp.stack([line, line ^ 1])
    chooser = ((lane[:, None] % slots == wanted[None, :]) & (lane[:, None] < 3 * slots)).astype(
        jnp.bfloat16
    )
    chip_weights = jnp.dot(all_weights, chooser, preferred_element_type=jnp.float32)
    chip_weights = chip_weights.reshape(len(offsets), local_tokens, 2)

    mine = (expert_gate[0], expert_up[0], expert_down[0])
    experts = (mine, tuple(partner(array, "line", 0) for array in mine))
    projections = ring_gather(out_proj)

    question_keys = question_key_values[:, :kv_columns]
    question_values = question_key_values[:, kv_columns:]
    own_pack = jnp.concatenate(
        [half(queries, member), both(question_keys, question_values, member)], axis=1
    )
    send_pack = jnp.concatenate(
        [half(queries, other), both(question_keys, question_values, other)], axis=1
    )
    both_pack = jnp.concatenate([own_pack, partner(send_pack, "line", 0)], axis=0)
    pair_rows = both_pack.shape[0]
    heads_of_queries = both_pack[:, :query_width].reshape(pair_rows, 1, heads_per_kv, HEAD_SIZE)
    local_keys = both_pack[:, query_width : query_width + HEAD_SIZE].reshape(pair_rows, 1, -1)
    local_values = both_pack[:, query_width + HEAD_SIZE :].reshape(pair_rows, 1, -1)
    start_state = near_state(heads_of_queries, local_keys, local_values, score_scale)
    run_max, run_sum, run_acc = fold_block(start_state, prefix, heads_of_queries, 1, score_scale)
    context = (run_acc / run_sum[..., None]).astype(jnp.bfloat16)

    by_parity = context.reshape(pair_rows, heads_per_kv // 2, 2, HEAD_SIZE)
    kept_heads = lax.dynamic_index_in_dim(by_parity, member, 2, keepdims=False)
    sent_heads = lax.dynamic_index_in_dim(by_parity, other, 2, keepdims=False)
    sent_heads = jnp.concatenate([sent_heads[local_tokens:], sent_heads[:local_tokens]], axis=0)
    heads = jnp.concatenate([kept_heads, partner(sent_heads, "line", 0)], axis=1)
    heads = heads.transpose(1, 0, 2)
    attended = 0.0
    for offset in sorted(projections, key=abs):
        pair = pair_at[(spot + offset) % pairs]
        place = (pair // (pairs // 2) ^ member) * (pairs // 2) + pair % (pairs // 2)
        attended = attended + jnp.dot(
            lax.dynamic_index_in_dim(heads, place, 0, keepdims=False),
            projections[offset],
            preferred_element_type=jnp.float32,
        )
    mixture = (
        residual_in.astype(jnp.float32)
        + attended[:local_tokens]
        + partner(attended[local_tokens:], "line", 0)
    )
    normed = (
        mixture * lax.rsqrt(jnp.mean(mixture * mixture, axis=-1, keepdims=True) + 1e-06) * norm_gain
    ).astype(jnp.bfloat16)

    rows = ring_gather(normed)
    answers = {}
    for step in range(1, pairs // 2 + 1):
        batch = [o for o in ((-step, step, 0) if step == 1 else (-step, step)) if o in rows]
        joined = jnp.concatenate([rows[o] for o in batch], axis=0)
        weights = jnp.concatenate([chip_weights[offsets.index(o)] for o in batch], axis=0)
        found = two_experts(joined, weights, experts)
        for number, o in enumerate(batch):
            answers[o] = found[number * local_tokens : (number + 1) * local_tokens]
    return (mixture + ring_sum(answers)).astype(jnp.bfloat16)


def solution(mesh):
    placed = (
        P(("group", "line"), None),
        P(("group", "line"), None),
        P(("group", "line"), None),
        P(("group", "line"), None),
        P("line", None),
        P(),
        P(("group", "line"), None),
        P(("group", "line"), None),
        P(("group", "line"), None),
        P(),
        P("line", None, None),
        P("line", None, None),
        P("line", None, None),
    )
    def whole(*arrays):
        tokens, experts = arrays[1].shape[0] // mesh.size, arrays[9].shape[0]
        dense = 2 * (tokens * TOPK // experts) >= tokens
        ring = dense and mesh.shape["line"] == QUERY_HEADS and experts == mesh.shape["line"]
        return jax.shard_map(
            ring_body if ring else body,
            mesh=mesh,
            in_specs=placed,
            out_specs=P(("group", "line"), None),
            check_vma=False,
        )(*arrays)

    return whole
```

```python
import functools
import math

import jax
import jax.numpy as jnp
from jax import lax
from jax.experimental import pallas as pl
from jax.experimental.pallas import tpu as pltpu
from jax.sharding import PartitionSpec as P


QUERY_HEADS = 16
KEY_VALUE_HEADS = 2
HEAD_SIZE = 128
TOPK = 8
QLEN = 16


def partner(array, axis, bit):
    return lax.ppermute(array, axis, [(i, i ^ 1 << bit) for i in range(lax.axis_size(axis))])


def shifted(value, axis, steps):
    count = lax.axis_size(axis)
    pairs = [(source, (source + steps) % count) for source in range(count)]
    return lax.ppermute(value, axis, pairs)


def expert_answers(received, expert_gate, expert_up, expert_down):
    buffer_shape = received.shape
    flat_rows = received.reshape(-1, buffer_shape[-1])
    gate_proj = jnp.dot(flat_rows, expert_gate[0], preferred_element_type=jnp.float32)
    upper = jnp.dot(flat_rows, expert_up[0], preferred_element_type=jnp.float32)
    middle = (jax.nn.silu(gate_proj) * upper).astype(jnp.bfloat16)
    return (
        jnp.dot(middle, expert_down[0], preferred_element_type=jnp.float32)
        .astype(jnp.bfloat16)
        .reshape(buffer_shape)
    )


def mix_experts(
    normed_rows,
    route_rows,
    keep_rows,
    weight_rows,
    expert_slots,
    expert_gate,
    expert_up,
    expert_down,
    slot_cap,
):
    row_count = normed_rows.shape[0]
    model_width = normed_rows.shape[1]
    line_count = lax.axis_size("line")
    pair_count = row_count * TOPK
    expert_ids = route_rows.reshape(pair_count)
    kept_pairs = keep_rows.reshape(pair_count) > 0
    numbers = jnp.arange(expert_slots.shape[0], dtype=jnp.int32)
    matches = expert_ids[:, None] == numbers[None, :]
    target = jnp.sum(jnp.where(matches, expert_slots[None, :], 0), axis=1)
    chosen = (matches & kept_pairs[:, None]).astype(jnp.bfloat16)
    pair_order = jnp.arange(pair_count, dtype=jnp.int32)
    earlier = (pair_order[:, None] > pair_order[None, :]).astype(jnp.bfloat16)
    before = jnp.dot(earlier, chosen, preferred_element_type=jnp.float32)
    slot_rank = jnp.sum(before * chosen.astype(jnp.float32), axis=1).astype(jnp.int32)
    slot_index = jnp.where(kept_pairs, target * slot_cap + slot_rank, line_count * slot_cap)
    slot_owner = (
        jnp.full((line_count * slot_cap,), pair_count, jnp.int32)
        .at[slot_index]
        .set(pair_order, mode="drop")
    )
    source_row = jnp.where(slot_owner < pair_count, slot_owner // TOPK, row_count)
    padded = jnp.concatenate([normed_rows, jnp.zeros((1, model_width), jnp.bfloat16)], axis=0)
    buffer = padded[source_row].reshape(line_count, slot_cap, model_width)
    returned = lax.all_to_all(
        expert_answers(
            lax.all_to_all(buffer, "line", split_axis=0, concat_axis=0, tiled=True),
            expert_gate,
            expert_up,
            expert_down,
        ),
        "line",
        split_axis=0,
        concat_axis=0,
        tiled=True,
    )
    padded_back = jnp.concatenate(
        [
            returned.reshape(line_count * slot_cap, model_width),
            jnp.zeros((1, model_width), jnp.bfloat16),
        ],
        axis=0,
    )
    per_pair = padded_back[slot_index].reshape(row_count, TOPK, model_width)
    weight = jnp.where(kept_pairs, weight_rows.reshape(pair_count), 0.0).reshape(row_count, TOPK)
    return jnp.sum(per_pair.astype(jnp.float32) * weight[:, :, None], axis=1)


def near_state(heads_of_queries, local_keys, local_values, score_scale):
    local_tokens = heads_of_queries.shape[0]
    near_scores = (
        jnp.einsum(
            "thgd,shd->thgs", heads_of_queries, local_keys, preferred_element_type=jnp.float32
        )
        * score_scale
    )
    position = jnp.arange(local_tokens, dtype=jnp.int32)
    visible_mask = (position[:, None] // QLEN == position[None, :] // QLEN) & (
        position[None, :] <= position[:, None]
    )
    near_scores = jnp.where(visible_mask[:, None, None, :], near_scores, -1e30)
    run_max = near_scores.max(-1)
    exp_terms = jnp.exp(near_scores - run_max[..., None])
    run_sum = exp_terms.sum(-1)
    run_acc = jnp.einsum(
        "thgs,shd->thgd",
        exp_terms.astype(jnp.bfloat16),
        local_values,
        preferred_element_type=jnp.float32,
    )
    return (run_max, run_sum, run_acc)


def fold_block(carry, piece, heads_of_queries, kv_heads, score_scale):
    old_max, old_sum, old_acc = carry
    piece_rows = piece.shape[0]
    piece_keys = piece[:, : kv_heads * HEAD_SIZE].reshape(piece_rows, kv_heads, HEAD_SIZE)
    piece_vals = piece[:, kv_heads * HEAD_SIZE :].reshape(piece_rows, kv_heads, HEAD_SIZE)
    far_scores = (
        jnp.einsum(
            "thgd,nhd->thgn", heads_of_queries, piece_keys, preferred_element_type=jnp.float32
        )
        * score_scale
    )
    new_max = jnp.maximum(old_max, far_scores.max(-1))
    factor = jnp.exp(old_max - new_max)
    far_terms = jnp.exp(far_scores - new_max[..., None])
    new_acc = old_acc * factor[..., None] + jnp.einsum(
        "thgn,nhd->thgd",
        far_terms.astype(jnp.bfloat16),
        piece_vals,
        preferred_element_type=jnp.float32,
    )
    return (new_max, old_sum * factor + far_terms.sum(-1), new_acc)


def body(
    residual_in,
    queries,
    question_key_values,
    document_prefix_cache,
    out_proj,
    norm_gain,
    routes,
    keep_mask,
    route_weights,
    expert_slots,
    expert_gate,
    expert_up,
    expert_down,
):
    local_tokens = queries.shape[0]
    queries_per_key_head = QUERY_HEADS // KEY_VALUE_HEADS
    score_scale = 1.0 / math.sqrt(HEAD_SIZE)
    half_kv = KEY_VALUE_HEADS // 2
    query_width = half_kv * queries_per_key_head * HEAD_SIZE
    kv_width = half_kv * HEAD_SIZE
    member = lax.axis_index("line") % 2
    other = 1 - member
    query_split = queries.reshape(local_tokens, 2, query_width)
    key_split = question_key_values[:, : KEY_VALUE_HEADS * HEAD_SIZE].reshape(
        local_tokens, 2, kv_width
    )
    value_split = question_key_values[:, KEY_VALUE_HEADS * HEAD_SIZE :].reshape(
        local_tokens, 2, kv_width
    )
    own_pack = jnp.concatenate(
        [
            lax.dynamic_index_in_dim(query_split, member, 1, keepdims=False),
            lax.dynamic_index_in_dim(key_split, member, 1, keepdims=False),
            lax.dynamic_index_in_dim(value_split, member, 1, keepdims=False),
        ],
        axis=1,
    )
    send_pack = jnp.concatenate(
        [
            lax.dynamic_index_in_dim(query_split, other, 1, keepdims=False),
            lax.dynamic_index_in_dim(key_split, other, 1, keepdims=False),
            lax.dynamic_index_in_dim(value_split, other, 1, keepdims=False),
        ],
        axis=1,
    )
    partner_pack = partner(send_pack, "line", 0)
    both_pack = jnp.concatenate([own_pack, partner_pack], axis=0)
    pair_rows = both_pack.shape[0]
    heads_of_queries = both_pack[:, :query_width].reshape(
        pair_rows, half_kv, queries_per_key_head, HEAD_SIZE
    )
    local_keys = both_pack[:, query_width : query_width + kv_width].reshape(
        pair_rows, half_kv, HEAD_SIZE
    )
    local_values = both_pack[:, query_width + kv_width :].reshape(pair_rows, half_kv, HEAD_SIZE)
    start_state = near_state(heads_of_queries, local_keys, local_values, score_scale)
    prefix_rows = document_prefix_cache.shape[0]
    document_keys = document_prefix_cache[:, : KEY_VALUE_HEADS * HEAD_SIZE].reshape(
        prefix_rows, 2, kv_width
    )
    document_values = document_prefix_cache[:, KEY_VALUE_HEADS * HEAD_SIZE :].reshape(
        prefix_rows, 2, kv_width
    )
    own_slab = jnp.concatenate(
        [
            lax.dynamic_index_in_dim(document_keys, member, 1, keepdims=False),
            lax.dynamic_index_in_dim(document_values, member, 1, keepdims=False),
        ],
        axis=1,
    )
    send_slab = jnp.concatenate(
        [
            lax.dynamic_index_in_dim(document_keys, other, 1, keepdims=False),
            lax.dynamic_index_in_dim(document_values, other, 1, keepdims=False),
        ],
        axis=1,
    )
    slab = jnp.concatenate([own_slab, partner(send_slab, "line", 0)], axis=0)
    levels = (lax.axis_size("line") // 2).bit_length() - 1
    for level in range(levels):
        slab = jnp.concatenate([slab, shifted(slab, "line", 2 * (1 << level))], axis=0)
    slab_rows = slab.shape[0]
    block_rows = math.gcd(slab_rows, 2048)
    slab_blocks = slab.reshape(slab_rows // block_rows, block_rows, 2 * kv_width)

    def scan_step(carry, piece):
        return (fold_block(carry, piece, heads_of_queries, half_kv, score_scale), None)

    final_state, _ = lax.scan(scan_step, start_state, slab_blocks)
    _, run_sum, run_acc = final_state
    pair_context = (
        (run_acc / run_sum[..., None]).reshape(pair_rows, query_width).astype(jnp.bfloat16)
    )
    mine = pair_context[:local_tokens]
    returned_context = partner(pair_context[local_tokens:], "line", 0)
    context_rows = jnp.where(
        member == 0,
        jnp.concatenate([mine, returned_context], axis=1),
        jnp.concatenate([returned_context, mine], axis=1),
    )
    attended = jnp.dot(
        context_rows,
        lax.all_gather(out_proj, "line", axis=0, tiled=True),
        preferred_element_type=jnp.float32,
    )
    mixture = residual_in.astype(jnp.float32) + attended
    normed = (
        mixture * lax.rsqrt(jnp.mean(mixture * mixture, axis=-1, keepdims=True) + 1e-06) * norm_gain
    ).astype(jnp.bfloat16)
    half_cap = local_tokens * TOPK // expert_slots.shape[0]
    expert_sum = mix_experts(
        normed,
        routes,
        keep_mask,
        route_weights,
        expert_slots,
        expert_gate,
        expert_up,
        expert_down,
        2 * half_cap,
    )
    return (mixture + expert_sum).astype(jnp.bfloat16)


def ring_spot(pair, pairs):
    row, column = divmod(pair, 2)
    return row if column == 0 else pairs - 1 - row


def ring_pair(spot, pairs):
    return 2 * spot if spot < pairs // 2 else 2 * (pairs - 1 - spot) + 1


def around(value, steps):
    count = lax.axis_size("line")
    pairs = count // 2
    moves = [
        (i, 2 * ring_pair((ring_spot(i // 2, pairs) + steps) % pairs, pairs) + i % 2)
        for i in range(count)
    ]
    return lax.ppermute(value, "line", moves)


def swap(value):
    return partner(value, "line", 0)


def ring_gather(value, halves):
    pairs = lax.axis_size("line") // 2
    last = pairs // 2
    cut = value.shape[0] // 2
    found = {0: value}
    for step in range(1, last):
        found[-step] = around(found[1 - step], 1)
        found[step] = around(found[step - 1], -1)
    if halves:
        found[-last] = (around(found[1 - last][:cut], 1), around(found[last - 1][cut:], -1))
    else:
        found[-last] = around(found[1 - last], 1)
    return found


def ring_sum(parts):
    pairs = len(parts)
    last = pairs // 2
    first_half, second_half = parts[-last]
    cut = first_half.shape[0]
    forward = around(first_half.astype(jnp.bfloat16), 1).astype(jnp.float32)
    backward = around(second_half.astype(jnp.bfloat16), -1).astype(jnp.float32)
    for step in range(2, last + 1):
        ahead = parts[last + 1 - step]
        behind = parts[step - last - 1]
        if step == 2:
            forward = jnp.concatenate([ahead[:cut] + forward, ahead[cut:]], axis=0)
            backward = jnp.concatenate([behind[:cut], behind[cut:] + backward], axis=0)
        else:
            forward = ahead + forward
            backward = behind + backward
        forward = around(forward.astype(jnp.bfloat16), 1).astype(jnp.float32)
        backward = around(backward.astype(jnp.bfloat16), -1).astype(jnp.float32)
    return parts[0] + forward + backward


def slot_weights(route_rows, keep_rows, weight_rows, expert_slots):
    numbers = jnp.arange(expert_slots.shape[0], dtype=jnp.int32)
    target = jnp.sum(
        jnp.where(route_rows[:, :, None] == numbers, expert_slots[None, None, :], 0), axis=2
    )
    kept = jnp.where(keep_rows > 0, weight_rows, 0.0)
    return jnp.sum(jnp.where(target[:, :, None] == numbers, kept[:, :, None], 0.0), axis=1)


def three_parts(values):
    high = lax.reduce_precision(values, 8, 7)
    rest = values - high
    middle = lax.reduce_precision(rest, 8, 7)
    return [part.astype(jnp.bfloat16) for part in (high, middle, rest - middle)]


def whole(shape):
    return pl.BlockSpec(shape, lambda *_: (0,) * len(shape))


def attention_kernel(prefix_rows, member_ref, *refs):
    own_ref, partner_ref = refs[:2]
    slab_refs, (kept_ref, sent_ref) = refs[2:-2], refs[-2:]
    tokens = own_ref.shape[0]
    rows = 2 * tokens
    scale = 1.0 / math.sqrt(HEAD_SIZE)
    query_width = own_ref.shape[1] - 2 * HEAD_SIZE
    contract_last = (((1,), (1,)), ((), ()))

    def columns(start):
        at = pl.ds(start, HEAD_SIZE)
        return jnp.concatenate([own_ref[:, at], partner_ref[:, at]], axis=0)

    near_keys = columns(query_width)
    near_values = columns(query_width + HEAD_SIZE)
    row = lax.broadcasted_iota(jnp.int32, (rows, rows), 0)
    column = lax.broadcasted_iota(jnp.int32, (rows, rows), 1)
    visible = (lax.div(row, QLEN) == lax.div(column, QLEN)) & (column <= row)

    def one_head(head):
        query = columns(pl.multiple_of(head * HEAD_SIZE, HEAD_SIZE))
        near = lax.dot_general(query, near_keys, contract_last, preferred_element_type=jnp.float32)
        scores = [jnp.where(visible, near * scale, -1e30)]
        values = [near_values]
        for slab_ref in slab_refs:
            keys = slab_ref[:prefix_rows, :HEAD_SIZE]
            far = lax.dot_general(query, keys, contract_last, preferred_element_type=jnp.float32)
            scores.append(far * scale)
            values.append(slab_ref[:prefix_rows, HEAD_SIZE:])
        largest = functools.reduce(
            jnp.maximum, [piece.max(axis=1, keepdims=True) for piece in scores]
        )
        total = jnp.zeros((rows, 1), jnp.float32)
        summed = jnp.zeros((rows, HEAD_SIZE), jnp.float32)
        for piece, value in zip(scores, values):
            terms = jnp.exp(piece - largest)
            total = total + terms.sum(axis=1, keepdims=True)
            summed = summed + jnp.dot(
                terms.astype(jnp.bfloat16), value, preferred_element_type=jnp.float32
            )
        return (summed / total).astype(jnp.bfloat16)

    def two_heads(number, carry):
        even, odd = one_head(2 * number), one_head(2 * number + 1)
        first = member_ref[0] == 0
        kept_ref[number] = jnp.where(first, even, odd)
        sent = jnp.where(first, odd, even)
        sent_ref[number] = jnp.concatenate([sent[tokens:], sent[:tokens]], axis=0)
        return carry

    lax.fori_loop(0, query_width // HEAD_SIZE // 2, two_heads, 0)


def attention(member, own_pack, partner_pack, slabs, prefix_rows):
    tokens, width = own_pack.shape
    half_heads = (width // HEAD_SIZE - 2) // 2
    shape = (half_heads, 2 * tokens, HEAD_SIZE)
    return pl.pallas_call(
        functools.partial(attention_kernel, prefix_rows),
        grid_spec=pltpu.PrefetchScalarGridSpec(
            num_scalar_prefetch=1,
            grid=(1,),
            in_specs=[whole(own_pack.shape)] * 2 + [whole(slabs[0].shape)] * len(slabs),
            out_specs=[whole(shape)] * 2,
        ),
        out_shape=[jax.ShapeDtypeStruct(shape, jnp.bfloat16)] * 2,
    )(member[None], own_pack, partner_pack, *slabs)


def project_kernel(numbers, carried, halved, place_ref, kept_ref, received_ref, *refs):
    start_refs = refs[: 2 * carried]
    weight_refs = refs[2 * carried : -2]
    out_refs = refs[-2:]
    half_heads = kept_ref.shape[0]
    tokens = out_refs[0].shape[0]

    def head(number):
        place = place_ref[number]
        inside = lax.rem(place, half_heads)
        return jnp.where(place < half_heads, kept_ref[inside], received_ref[inside])

    total = jnp.zeros((2 * tokens, out_refs[0].shape[1]), jnp.float32)
    at = 0
    for number in numbers:
        rows = head(number)
        if number == halved:
            cut = weight_refs[at].shape[0]
            for begin in (0, cut):
                total = total + jnp.dot(
                    rows[:, begin : begin + cut],
                    weight_refs[at][...],
                    preferred_element_type=jnp.float32,
                )
                at += 1
        else:
            total = total + jnp.dot(
                rows, weight_refs[at][...], preferred_element_type=jnp.float32
            )
            at += 1
    for place, out_ref in enumerate(out_refs):
        piece = total[place * tokens : (place + 1) * tokens]
        out_ref[...] = piece + start_refs[place][...] if carried else piece


def project(places, numbers, kept, received, starts, weights, halved):
    flat = []
    for weight in weights:
        flat.extend(weight if isinstance(weight, tuple) else (weight,))
    shape = (kept.shape[1] // 2, flat[0].shape[1])
    arrays = [kept, received, *starts, *flat]
    return pl.pallas_call(
        functools.partial(project_kernel, numbers, bool(starts), halved),
        grid_spec=pltpu.PrefetchScalarGridSpec(
            num_scalar_prefetch=1,
            grid=(1,),
            in_specs=[whole(array.shape) for array in arrays],
            out_specs=[whole(shape)] * 2,
        ),
        out_shape=[jax.ShapeDtypeStruct(shape, jnp.float32)] * 2,
    )(places, *arrays)


def norm_kernel(residual_ref, mine_ref, theirs_ref, gain_ref, mixture_ref, normed_ref):
    mixture = residual_ref[...].astype(jnp.float32) + mine_ref[...] + theirs_ref[...]
    mixture_ref[...] = mixture
    mean = jnp.mean(mixture * mixture, axis=-1, keepdims=True)
    normed_ref[...] = (mixture * lax.rsqrt(mean + 1e-06) * gain_ref[...]).astype(jnp.bfloat16)


def expert_kernel(count, chosen, carried, *refs):
    row_refs, refs = refs[:count], refs[count:]
    share_ref, refs = refs[0], refs[1:]
    start_refs, refs = refs[: count * carried], refs[count * carried :]
    weight_refs, refs = refs[: 3 * len(chosen)], refs[3 * len(chosen) :]
    out_refs, (rows, answer, total) = refs[:-3], refs[-3:]
    expert, tile = pl.program_id(0), pl.program_id(1)
    tiles = pl.num_programs(1)
    places = [0]
    for row_ref in row_refs:
        places.append(places[-1] + row_ref.shape[0])

    @pl.when((expert == 0) & (tile == 0))
    def _():
        for number, row_ref in enumerate(row_refs):
            rows[places[number] : places[number + 1], :] = row_ref[...]

    def work(number):
        gate_ref, up_ref, down_ref = weight_refs[3 * number : 3 * number + 3]
        taken = rows[...]
        gate = jnp.dot(taken, gate_ref[...], preferred_element_type=jnp.float32)
        upper = jnp.dot(taken, up_ref[...], preferred_element_type=jnp.float32)
        middle = (gate / (1.0 + jnp.exp(-gate)) * upper).astype(jnp.bfloat16)
        piece = jnp.dot(middle, down_ref[...], preferred_element_type=jnp.float32)

        @pl.when(tile == 0)
        def _():
            answer[...] = piece

        @pl.when((tile > 0) & (tile < tiles - 1))
        def _():
            answer[...] += piece

        @pl.when(tile == tiles - 1)
        def _():
            done = piece + answer[...] if tiles > 1 else piece
            rounded = done.astype(jnp.bfloat16).astype(jnp.float32)
            column = chosen[number]
            result = rounded * share_ref[:, column : column + 1]
            if number > 0:
                result = result + total[...]
            if number < len(chosen) - 1:
                total[...] = result
                return None
            begin = 0
            for place, out_ref in enumerate(out_refs):
                piece_rows = result[begin : begin + out_ref.shape[0]]
                begin += out_ref.shape[0]
                if carried:
                    piece_rows = piece_rows + start_refs[place][...]
                out_ref[...] = piece_rows.astype(out_ref.dtype)

    for number in range(len(chosen)):
        pl.when(expert == number)(functools.partial(work, number))


def run_experts(pieces, shares, experts, chosen, starts, split):
    width = pieces[0].shape[1]
    hidden = experts[0][0].shape[1]
    tile = 256 if hidden % 256 == 0 else hidden
    tiles = hidden // tile
    row_count = sum(piece.shape[0] for piece in pieces)
    weight_specs, weights = [], []
    for number, expert in enumerate(chosen):

        def step(e, t, number=number):
            return jnp.where(e == number, t, jnp.where(e < number, 0, tiles - 1))

        weight_specs += [pl.BlockSpec((width, tile), lambda e, t, step=step: (0, step(e, t)))] * 2
        weight_specs += [pl.BlockSpec((tile, width), lambda e, t, step=step: (step(e, t), 0))]
        weights += experts[expert]
    arrays = [*pieces, shares, *starts]
    results = [jax.ShapeDtypeStruct(piece.shape, jnp.float32) for piece in pieces]
    if split:
        halved = (pieces[0].shape[0] // 2, width)
        results[:1] = [jax.ShapeDtypeStruct(halved, jnp.bfloat16)] * 2
    return pl.pallas_call(
        functools.partial(expert_kernel, len(pieces), chosen, bool(starts)),
        grid=(len(chosen), tiles),
        in_specs=[whole(array.shape) for array in arrays] + weight_specs,
        out_specs=[whole(result.shape) for result in results],
        out_shape=results,
        scratch_shapes=[
            pltpu.VMEM((row_count, width), jnp.bfloat16),
            pltpu.VMEM((row_count, width), jnp.float32),
            pltpu.VMEM((row_count, width), jnp.float32),
        ],
        compiler_params=pltpu.CompilerParams(vmem_limit_bytes=56 << 20),
    )(*arrays, *weights)


def ring_body(
    residual_in,
    queries,
    question_key_values,
    document_prefix_cache,
    out_proj,
    norm_gain,
    routes,
    keep_mask,
    route_weights,
    expert_slots,
    expert_gate,
    expert_up,
    expert_down,
):
    local_tokens = queries.shape[0]
    line = lax.axis_index("line")
    lines = lax.axis_size("line")
    pairs = lines // 2
    last = pairs // 2
    member = line & 1
    other = 1 - member
    offsets = list(range(-last, pairs - last))

    table = []
    for device in range(lines):
        spot = ring_spot(device // 2, pairs)
        held = [ring_pair((spot + offset) % pairs, pairs) for offset in offsets]
        table.append([(pair // last ^ device % 2) * last + pair % last for pair in held])
    places = lax.dynamic_index_in_dim(jnp.array(table, jnp.int32), line, 0, keepdims=False)

    def half(array, which):
        return lax.dynamic_slice_in_dim(
            array, which * (array.shape[1] // 2), array.shape[1] // 2, axis=1
        )

    def both(left, right, which):
        return jnp.concatenate([half(left, which), half(right, which)], axis=1)

    projections = ring_gather(out_proj, True)

    kv_columns = KEY_VALUE_HEADS * HEAD_SIZE
    prefix_keys = document_prefix_cache[:, :kv_columns]
    prefix_values = document_prefix_cache[:, kv_columns:]
    slab = jnp.concatenate(
        [
            both(prefix_keys, prefix_values, member),
            swap(both(prefix_keys, prefix_values, other)),
        ],
        axis=0,
    )
    slots = expert_slots.shape[0]
    pieces = three_parts(slot_weights(routes, keep_mask, route_weights, expert_slots).T)
    pieces.append(jnp.zeros((slots, 2 * HEAD_SIZE - 3 * local_tokens), jnp.bfloat16))
    arrived = ring_gather(jnp.concatenate([slab, jnp.concatenate(pieces, axis=1)], axis=0), False)
    prefix_rows = slab.shape[0]
    wanted = jnp.stack([line, line ^ 1])
    chooser = (jnp.arange(slots, dtype=jnp.int32)[:, None] == wanted[None, :]).astype(jnp.bfloat16)

    def shares(batch):
        blocks = jnp.concatenate(
            [
                arrived[o][prefix_rows:, part * local_tokens : (part + 1) * local_tokens]
                for part in range(3)
                for o in batch
            ],
            axis=1,
        )
        found = lax.dot_general(
            blocks, chooser, (((0,), (0,)), ((), ())), preferred_element_type=jnp.float32
        )
        return found.reshape(3, len(batch) * local_tokens, 2).sum(axis=0)

    mine = (expert_gate[0], expert_up[0], expert_down[0])
    experts = (mine, tuple(swap(array) for array in mine))

    question_keys = question_key_values[:, :kv_columns]
    question_values = question_key_values[:, kv_columns:]
    own_pack = jnp.concatenate(
        [half(queries, member), both(question_keys, question_values, member)], axis=1
    )
    send_pack = jnp.concatenate(
        [half(queries, other), both(question_keys, question_values, other)], axis=1
    )
    kept, sent = attention(
        member,
        own_pack,
        swap(send_pack),
        [arrived[o] for o in offsets],
        prefix_rows,
    )

    early = [o for o in offsets if abs(o) < last - 1]
    late = [o for o in offsets if abs(o) >= last - 1]
    sent, places, shares_early, shares_late = lax.optimization_barrier(
        (sent, places, shares(early), shares(late))
    )
    received = swap(sent)

    def projected(batch, starts):
        numbers = tuple(offsets.index(o) for o in batch)
        return project(
            places,
            numbers,
            kept,
            received,
            starts,
            [projections[o] for o in batch],
            offsets.index(-last),
        )

    for_me, for_partner = projected(late, projected(early, []))
    shape = residual_in.shape
    mixture, normed = pl.pallas_call(
        norm_kernel,
        out_shape=[
            jax.ShapeDtypeStruct(shape, jnp.float32),
            jax.ShapeDtypeStruct(shape, jnp.bfloat16),
        ],
    )(residual_in, for_me, swap(for_partner), norm_gain[None, :])

    rows = ring_gather(normed, False)
    answers = [[] for _ in early]
    for number in range(2):
        answers = run_experts(
            [rows[o] for o in early],
            shares_early,
            experts,
            (number,),
            answers if number else [],
            False,
        )
    parts = dict(zip(early, answers))
    found = run_experts([rows[o] for o in late], shares_late, experts, (0, 1), [], True)
    parts[-last] = tuple(found[:2])
    parts.update(zip(late[1:], found[2:]))
    return (mixture + ring_sum(parts)).astype(jnp.bfloat16)


def solution(mesh):
    placed = (
        P(("group", "line"), None),
        P(("group", "line"), None),
        P(("group", "line"), None),
        P(("group", "line"), None),
        P("line", None),
        P(),
        P(("group", "line"), None),
        P(("group", "line"), None),
        P(("group", "line"), None),
        P(),
        P("line", None, None),
        P("line", None, None),
        P("line", None, None),
    )

    tokens_of = lambda arrays: arrays[1].shape[0] // mesh.size

    def layer(*arrays):
        tokens, experts = tokens_of(arrays), arrays[9].shape[0]
        dense = 2 * (tokens * TOPK // experts) >= tokens
        ring = dense and mesh.shape["line"] == QUERY_HEADS and experts == mesh.shape["line"]
        return jax.shard_map(
            ring_body if ring else body,
            mesh=mesh,
            in_specs=placed,
            out_specs=P(("group", "line"), None),
            check_vma=False,
        )(*arrays)

    return layer
```

```python
import functools
import math

import jax
import jax.numpy as jnp
from jax import lax
from jax.experimental import pallas as pl
from jax.experimental.pallas import tpu as pltpu
from jax.sharding import PartitionSpec as P


QUERY_HEADS = 16
KEY_VALUE_HEADS = 2
HEAD_SIZE = 128
TOPK = 8
QLEN = 16


def partner(array, axis, bit):
    return lax.ppermute(array, axis, [(i, i ^ 1 << bit) for i in range(lax.axis_size(axis))])


def shifted(value, axis, steps):
    count = lax.axis_size(axis)
    pairs = [(source, (source + steps) % count) for source in range(count)]
    return lax.ppermute(value, axis, pairs)


def expert_answers(received, expert_gate, expert_up, expert_down):
    buffer_shape = received.shape
    flat_rows = received.reshape(-1, buffer_shape[-1])
    gate_proj = jnp.dot(flat_rows, expert_gate[0], preferred_element_type=jnp.float32)
    upper = jnp.dot(flat_rows, expert_up[0], preferred_element_type=jnp.float32)
    middle = (jax.nn.silu(gate_proj) * upper).astype(jnp.bfloat16)
    return (
        jnp.dot(middle, expert_down[0], preferred_element_type=jnp.float32)
        .astype(jnp.bfloat16)
        .reshape(buffer_shape)
    )


def mix_experts(
    normed_rows,
    route_rows,
    keep_rows,
    weight_rows,
    expert_slots,
    expert_gate,
    expert_up,
    expert_down,
    slot_cap,
):
    row_count = normed_rows.shape[0]
    model_width = normed_rows.shape[1]
    line_count = lax.axis_size("line")
    pair_count = row_count * TOPK
    expert_ids = route_rows.reshape(pair_count)
    kept_pairs = keep_rows.reshape(pair_count) > 0
    numbers = jnp.arange(expert_slots.shape[0], dtype=jnp.int32)
    matches = expert_ids[:, None] == numbers[None, :]
    target = jnp.sum(jnp.where(matches, expert_slots[None, :], 0), axis=1)
    chosen = (matches & kept_pairs[:, None]).astype(jnp.bfloat16)
    pair_order = jnp.arange(pair_count, dtype=jnp.int32)
    earlier = (pair_order[:, None] > pair_order[None, :]).astype(jnp.bfloat16)
    before = jnp.dot(earlier, chosen, preferred_element_type=jnp.float32)
    slot_rank = jnp.sum(before * chosen.astype(jnp.float32), axis=1).astype(jnp.int32)
    slot_index = jnp.where(kept_pairs, target * slot_cap + slot_rank, line_count * slot_cap)
    slot_owner = (
        jnp.full((line_count * slot_cap,), pair_count, jnp.int32)
        .at[slot_index]
        .set(pair_order, mode="drop")
    )
    source_row = jnp.where(slot_owner < pair_count, slot_owner // TOPK, row_count)
    padded = jnp.concatenate([normed_rows, jnp.zeros((1, model_width), jnp.bfloat16)], axis=0)
    buffer = padded[source_row].reshape(line_count, slot_cap, model_width)
    returned = lax.all_to_all(
        expert_answers(
            lax.all_to_all(buffer, "line", split_axis=0, concat_axis=0, tiled=True),
            expert_gate,
            expert_up,
            expert_down,
        ),
        "line",
        split_axis=0,
        concat_axis=0,
        tiled=True,
    )
    padded_back = jnp.concatenate(
        [
            returned.reshape(line_count * slot_cap, model_width),
            jnp.zeros((1, model_width), jnp.bfloat16),
        ],
        axis=0,
    )
    per_pair = padded_back[slot_index].reshape(row_count, TOPK, model_width)
    weight = jnp.where(kept_pairs, weight_rows.reshape(pair_count), 0.0).reshape(row_count, TOPK)
    return jnp.sum(per_pair.astype(jnp.float32) * weight[:, :, None], axis=1)


def near_state(heads_of_queries, local_keys, local_values, score_scale):
    local_tokens = heads_of_queries.shape[0]
    near_scores = (
        jnp.einsum(
            "thgd,shd->thgs", heads_of_queries, local_keys, preferred_element_type=jnp.float32
        )
        * score_scale
    )
    position = jnp.arange(local_tokens, dtype=jnp.int32)
    visible_mask = (position[:, None] // QLEN == position[None, :] // QLEN) & (
        position[None, :] <= position[:, None]
    )
    near_scores = jnp.where(visible_mask[:, None, None, :], near_scores, -1e30)
    run_max = near_scores.max(-1)
    exp_terms = jnp.exp(near_scores - run_max[..., None])
    run_sum = exp_terms.sum(-1)
    run_acc = jnp.einsum(
        "thgs,shd->thgd",
        exp_terms.astype(jnp.bfloat16),
        local_values,
        preferred_element_type=jnp.float32,
    )
    return (run_max, run_sum, run_acc)


def fold_block(carry, piece, heads_of_queries, kv_heads, score_scale):
    old_max, old_sum, old_acc = carry
    piece_rows = piece.shape[0]
    piece_keys = piece[:, : kv_heads * HEAD_SIZE].reshape(piece_rows, kv_heads, HEAD_SIZE)
    piece_vals = piece[:, kv_heads * HEAD_SIZE :].reshape(piece_rows, kv_heads, HEAD_SIZE)
    far_scores = (
        jnp.einsum(
            "thgd,nhd->thgn", heads_of_queries, piece_keys, preferred_element_type=jnp.float32
        )
        * score_scale
    )
    new_max = jnp.maximum(old_max, far_scores.max(-1))
    factor = jnp.exp(old_max - new_max)
    far_terms = jnp.exp(far_scores - new_max[..., None])
    new_acc = old_acc * factor[..., None] + jnp.einsum(
        "thgn,nhd->thgd",
        far_terms.astype(jnp.bfloat16),
        piece_vals,
        preferred_element_type=jnp.float32,
    )
    return (new_max, old_sum * factor + far_terms.sum(-1), new_acc)


def body(
    residual_in,
    queries,
    question_key_values,
    document_prefix_cache,
    out_proj,
    norm_gain,
    routes,
    keep_mask,
    route_weights,
    expert_slots,
    expert_gate,
    expert_up,
    expert_down,
):
    local_tokens = queries.shape[0]
    queries_per_key_head = QUERY_HEADS // KEY_VALUE_HEADS
    score_scale = 1.0 / math.sqrt(HEAD_SIZE)
    half_kv = KEY_VALUE_HEADS // 2
    query_width = half_kv * queries_per_key_head * HEAD_SIZE
    kv_width = half_kv * HEAD_SIZE
    member = lax.axis_index("line") % 2
    other = 1 - member
    query_split = queries.reshape(local_tokens, 2, query_width)
    key_split = question_key_values[:, : KEY_VALUE_HEADS * HEAD_SIZE].reshape(
        local_tokens, 2, kv_width
    )
    value_split = question_key_values[:, KEY_VALUE_HEADS * HEAD_SIZE :].reshape(
        local_tokens, 2, kv_width
    )
    own_pack = jnp.concatenate(
        [
            lax.dynamic_index_in_dim(query_split, member, 1, keepdims=False),
            lax.dynamic_index_in_dim(key_split, member, 1, keepdims=False),
            lax.dynamic_index_in_dim(value_split, member, 1, keepdims=False),
        ],
        axis=1,
    )
    send_pack = jnp.concatenate(
        [
            lax.dynamic_index_in_dim(query_split, other, 1, keepdims=False),
            lax.dynamic_index_in_dim(key_split, other, 1, keepdims=False),
            lax.dynamic_index_in_dim(value_split, other, 1, keepdims=False),
        ],
        axis=1,
    )
    partner_pack = partner(send_pack, "line", 0)
    both_pack = jnp.concatenate([own_pack, partner_pack], axis=0)
    pair_rows = both_pack.shape[0]
    heads_of_queries = both_pack[:, :query_width].reshape(
        pair_rows, half_kv, queries_per_key_head, HEAD_SIZE
    )
    local_keys = both_pack[:, query_width : query_width + kv_width].reshape(
        pair_rows, half_kv, HEAD_SIZE
    )
    local_values = both_pack[:, query_width + kv_width :].reshape(pair_rows, half_kv, HEAD_SIZE)
    start_state = near_state(heads_of_queries, local_keys, local_values, score_scale)
    prefix_rows = document_prefix_cache.shape[0]
    document_keys = document_prefix_cache[:, : KEY_VALUE_HEADS * HEAD_SIZE].reshape(
        prefix_rows, 2, kv_width
    )
    document_values = document_prefix_cache[:, KEY_VALUE_HEADS * HEAD_SIZE :].reshape(
        prefix_rows, 2, kv_width
    )
    own_slab = jnp.concatenate(
        [
            lax.dynamic_index_in_dim(document_keys, member, 1, keepdims=False),
            lax.dynamic_index_in_dim(document_values, member, 1, keepdims=False),
        ],
        axis=1,
    )
    send_slab = jnp.concatenate(
        [
            lax.dynamic_index_in_dim(document_keys, other, 1, keepdims=False),
            lax.dynamic_index_in_dim(document_values, other, 1, keepdims=False),
        ],
        axis=1,
    )
    slab = jnp.concatenate([own_slab, partner(send_slab, "line", 0)], axis=0)
    levels = (lax.axis_size("line") // 2).bit_length() - 1
    for level in range(levels):
        slab = jnp.concatenate([slab, shifted(slab, "line", 2 * (1 << level))], axis=0)
    slab_rows = slab.shape[0]
    block_rows = math.gcd(slab_rows, 2048)
    slab_blocks = slab.reshape(slab_rows // block_rows, block_rows, 2 * kv_width)

    def scan_step(carry, piece):
        return (fold_block(carry, piece, heads_of_queries, half_kv, score_scale), None)

    final_state, _ = lax.scan(scan_step, start_state, slab_blocks)
    _, run_sum, run_acc = final_state
    pair_context = (
        (run_acc / run_sum[..., None]).reshape(pair_rows, query_width).astype(jnp.bfloat16)
    )
    mine = pair_context[:local_tokens]
    returned_context = partner(pair_context[local_tokens:], "line", 0)
    context_rows = jnp.where(
        member == 0,
        jnp.concatenate([mine, returned_context], axis=1),
        jnp.concatenate([returned_context, mine], axis=1),
    )
    attended = jnp.dot(
        context_rows,
        lax.all_gather(out_proj, "line", axis=0, tiled=True),
        preferred_element_type=jnp.float32,
    )
    mixture = residual_in.astype(jnp.float32) + attended
    normed = (
        mixture * lax.rsqrt(jnp.mean(mixture * mixture, axis=-1, keepdims=True) + 1e-06) * norm_gain
    ).astype(jnp.bfloat16)
    half_cap = local_tokens * TOPK // expert_slots.shape[0]
    expert_sum = mix_experts(
        normed,
        routes,
        keep_mask,
        route_weights,
        expert_slots,
        expert_gate,
        expert_up,
        expert_down,
        2 * half_cap,
    )
    return (mixture + expert_sum).astype(jnp.bfloat16)


def ring_spot(pair, pairs):
    row, column = divmod(pair, 2)
    return row if column == 0 else pairs - 1 - row


def ring_pair(spot, pairs):
    return 2 * spot if spot < pairs // 2 else 2 * (pairs - 1 - spot) + 1


def around(value, steps):
    count = lax.axis_size("line")
    pairs = count // 2
    moves = [
        (i, 2 * ring_pair((ring_spot(i // 2, pairs) + steps) % pairs, pairs) + i % 2)
        for i in range(count)
    ]
    return lax.ppermute(value, "line", moves)


def swap(value):
    return partner(value, "line", 0)


def ring_gather(value, halves):
    pairs = lax.axis_size("line") // 2
    last = pairs // 2
    cut = value.shape[0] // 2
    found = {0: value}
    for step in range(1, last):
        found[-step] = around(found[1 - step], 1)
        found[step] = around(found[step - 1], -1)
    if halves:
        found[-last] = (around(found[1 - last][:cut], 1), around(found[last - 1][cut:], -1))
    else:
        found[-last] = around(found[1 - last], 1)
    return found


def ring_sum(parts):
    pairs = len(parts)
    last = pairs // 2
    first_half, second_half = parts[-last]
    cut = first_half.shape[0]
    forward = around(first_half.astype(jnp.bfloat16), 1).astype(jnp.float32)
    backward = around(second_half.astype(jnp.bfloat16), -1).astype(jnp.float32)
    for step in range(2, last + 1):
        ahead = parts[last + 1 - step]
        behind = parts[step - last - 1]
        if step == 2:
            forward = jnp.concatenate([ahead[:cut] + forward, ahead[cut:]], axis=0)
            backward = jnp.concatenate([behind[:cut], behind[cut:] + backward], axis=0)
        else:
            forward = ahead + forward
            backward = behind + backward
        forward = around(forward.astype(jnp.bfloat16), 1).astype(jnp.float32)
        backward = around(backward.astype(jnp.bfloat16), -1).astype(jnp.float32)
    return parts[0] + forward + backward


def slot_weights(route_rows, keep_rows, weight_rows, expert_slots):
    numbers = jnp.arange(expert_slots.shape[0], dtype=jnp.int32)
    target = jnp.sum(
        jnp.where(route_rows[:, :, None] == numbers, expert_slots[None, None, :], 0), axis=2
    )
    kept = jnp.where(keep_rows > 0, weight_rows, 0.0)
    return jnp.sum(jnp.where(target[:, :, None] == numbers, kept[:, :, None], 0.0), axis=1)


def three_parts(values):
    high = lax.reduce_precision(values, 8, 7)
    rest = values - high
    middle = lax.reduce_precision(rest, 8, 7)
    return [part.astype(jnp.bfloat16) for part in (high, middle, rest - middle)]


def whole(shape):
    return pl.BlockSpec(shape, lambda *_: (0,) * len(shape))


def attention_kernel(prefix_rows, member_ref, *refs):
    own_ref, partner_ref, chooser_ref = refs[:3]
    slab_refs, (kept_ref, sent_ref, share_ref) = refs[3:-3], refs[-3:]
    tokens = own_ref.shape[0]
    chooser = chooser_ref[...]
    for number, slab_ref in enumerate(slab_refs):
        found = None
        for part in range(3):
            block = slab_ref[prefix_rows:, part * tokens : (part + 1) * tokens]
            piece = lax.dot_general(
                block, chooser, (((0,), (0,)), ((), ())), preferred_element_type=jnp.float32
            )
            found = piece if found is None else found + piece
        share_ref[number] = found
    rows = 2 * tokens
    scale = 1.0 / math.sqrt(HEAD_SIZE)
    query_width = own_ref.shape[1] - 2 * HEAD_SIZE
    contract_last = (((1,), (1,)), ((), ()))

    def columns(start):
        at = pl.ds(start, HEAD_SIZE)
        return jnp.concatenate([own_ref[:, at], partner_ref[:, at]], axis=0)

    near_keys = columns(query_width)
    near_values = columns(query_width + HEAD_SIZE)
    row = lax.broadcasted_iota(jnp.int32, (rows, rows), 0)
    column = lax.broadcasted_iota(jnp.int32, (rows, rows), 1)
    visible = (lax.div(row, QLEN) == lax.div(column, QLEN)) & (column <= row)

    def one_head(head):
        query = columns(pl.multiple_of(head * HEAD_SIZE, HEAD_SIZE))
        near = lax.dot_general(query, near_keys, contract_last, preferred_element_type=jnp.float32)
        scores = [jnp.where(visible, near * scale, -1e30)]
        values = [near_values]
        for slab_ref in slab_refs:
            keys = slab_ref[:prefix_rows, :HEAD_SIZE]
            far = lax.dot_general(query, keys, contract_last, preferred_element_type=jnp.float32)
            scores.append(far * scale)
            values.append(slab_ref[:prefix_rows, HEAD_SIZE:])
        largest = functools.reduce(
            jnp.maximum, [piece.max(axis=1, keepdims=True) for piece in scores]
        )
        total = jnp.zeros((rows, 1), jnp.float32)
        summed = jnp.zeros((rows, HEAD_SIZE), jnp.float32)
        for piece, value in zip(scores, values):
            terms = jnp.exp(piece - largest)
            total = total + terms.sum(axis=1, keepdims=True)
            summed = summed + jnp.dot(
                terms.astype(jnp.bfloat16), value, preferred_element_type=jnp.float32
            )
        return (summed / total).astype(jnp.bfloat16)

    def two_heads(number, carry):
        even, odd = one_head(2 * number), one_head(2 * number + 1)
        first = member_ref[0] == 0
        kept_ref[number] = jnp.where(first, even, odd)
        sent = jnp.where(first, odd, even)
        sent_ref[number] = jnp.concatenate([sent[tokens:], sent[:tokens]], axis=0)
        return carry

    lax.fori_loop(0, query_width // HEAD_SIZE // 2, two_heads, 0)


def attention(member, own_pack, partner_pack, chooser, slabs, prefix_rows):
    tokens, width = own_pack.shape
    half_heads = (width // HEAD_SIZE - 2) // 2
    shape = (half_heads, 2 * tokens, HEAD_SIZE)
    share_shape = (len(slabs), tokens, 2)
    arrays = [own_pack, partner_pack, chooser, *slabs]
    return pl.pallas_call(
        functools.partial(attention_kernel, prefix_rows),
        grid_spec=pltpu.PrefetchScalarGridSpec(
            num_scalar_prefetch=1,
            grid=(1,),
            in_specs=[whole(array.shape) for array in arrays],
            out_specs=[whole(shape)] * 2 + [whole(share_shape)],
        ),
        out_shape=[jax.ShapeDtypeStruct(shape, jnp.bfloat16)] * 2
        + [jax.ShapeDtypeStruct(share_shape, jnp.float32)],
    )(member[None], *arrays)


def project_kernel(numbers, carried, halved, place_ref, kept_ref, received_ref, *refs):
    start_refs = refs[: 2 * carried]
    weight_refs = refs[2 * carried : -2]
    out_refs = refs[-2:]
    half_heads = kept_ref.shape[0]
    tokens = out_refs[0].shape[0]

    def head(number):
        place = place_ref[number]
        inside = lax.rem(place, half_heads)
        return jnp.where(place < half_heads, kept_ref[inside], received_ref[inside])

    total = jnp.zeros((2 * tokens, out_refs[0].shape[1]), jnp.float32)
    at = 0
    for number in numbers:
        rows = head(number)
        if number == halved:
            cut = weight_refs[at].shape[0]
            for begin in (0, cut):
                total = total + jnp.dot(
                    rows[:, begin : begin + cut],
                    weight_refs[at][...],
                    preferred_element_type=jnp.float32,
                )
                at += 1
        else:
            total = total + jnp.dot(
                rows, weight_refs[at][...], preferred_element_type=jnp.float32
            )
            at += 1
    for place, out_ref in enumerate(out_refs):
        piece = total[place * tokens : (place + 1) * tokens]
        out_ref[...] = piece + start_refs[place][...] if carried else piece


def project(places, numbers, kept, received, starts, weights, halved):
    flat = []
    for weight in weights:
        flat.extend(weight if isinstance(weight, tuple) else (weight,))
    shape = (kept.shape[1] // 2, flat[0].shape[1])
    arrays = [kept, received, *starts, *flat]
    return pl.pallas_call(
        functools.partial(project_kernel, numbers, bool(starts), halved),
        grid_spec=pltpu.PrefetchScalarGridSpec(
            num_scalar_prefetch=1,
            grid=(1,),
            in_specs=[whole(array.shape) for array in arrays],
            out_specs=[whole(shape)] * 2,
        ),
        out_shape=[jax.ShapeDtypeStruct(shape, jnp.float32)] * 2,
        compiler_params=pltpu.CompilerParams(vmem_limit_bytes=16 << 20),
    )(places, *arrays)


def norm_kernel(residual_ref, mine_ref, theirs_ref, gain_ref, mixture_ref, normed_ref):
    mixture = residual_ref[...].astype(jnp.float32) + mine_ref[...] + theirs_ref[...]
    mixture_ref[...] = mixture
    mean = jnp.mean(mixture * mixture, axis=-1, keepdims=True)
    normed_ref[...] = (mixture * lax.rsqrt(mean + 1e-06) * gain_ref[...]).astype(jnp.bfloat16)


def expert_kernel(count, places, *refs):
    row_refs, share_ref, weight_refs, out_refs = (
        refs[:count],
        refs[count],
        refs[count + 1 : count + 7],
        refs[count + 7 :],
    )
    rows = jnp.concatenate([row_ref[...] for row_ref in row_refs], axis=0)
    hidden = weight_refs[0].shape[1]
    tile = 256 if hidden % 256 == 0 else hidden
    result = None
    for number in range(2):
        gate_ref, up_ref, down_ref = weight_refs[3 * number : 3 * number + 3]
        answer = None
        for begin in range(0, hidden, tile):
            inside = slice(begin, begin + tile)
            gate = jnp.dot(rows, gate_ref[:, inside], preferred_element_type=jnp.float32)
            upper = jnp.dot(rows, up_ref[:, inside], preferred_element_type=jnp.float32)
            middle = (gate / (1.0 + jnp.exp(-gate)) * upper).astype(jnp.bfloat16)
            piece = jnp.dot(middle, down_ref[inside, :], preferred_element_type=jnp.float32)
            answer = piece if answer is None else answer + piece
        rounded = answer.astype(jnp.bfloat16).astype(jnp.float32)
        share = jnp.concatenate([share_ref[n, :, number : number + 1] for n in places], axis=0)
        weighted = rounded * share
        result = weighted if result is None else result + weighted
    begin = 0
    for out_ref in out_refs:
        out_ref[...] = result[begin : begin + out_ref.shape[0]].astype(out_ref.dtype)
        begin += out_ref.shape[0]


def load_kernel(*refs):
    count = len(refs) // 2
    copies = [
        pltpu.make_async_copy(refs[n], refs[count + n], refs[2 * count].at[n])
        for n in range(count)
    ]
    for copy in copies:
        copy.start()
    for copy in copies:
        copy.wait()


def load(arrays):
    return pl.pallas_call(
        load_kernel,
        in_specs=[pl.BlockSpec(memory_space=pl.ANY)] * len(arrays),
        out_specs=[pl.BlockSpec(memory_space=pltpu.VMEM)] * len(arrays),
        out_shape=[jax.ShapeDtypeStruct(array.shape, array.dtype) for array in arrays],
        scratch_shapes=[pltpu.SemaphoreType.DMA((len(arrays),))],
        compiler_params=pltpu.CompilerParams(vmem_limit_bytes=16 << 20),
    )(*arrays)


def run_experts(pieces, shares, places, experts, split):
    results = [jax.ShapeDtypeStruct(piece.shape, jnp.float32) for piece in pieces]
    if split:
        halved = (pieces[0].shape[0] // 2, pieces[0].shape[1])
        results[:1] = [jax.ShapeDtypeStruct(halved, jnp.bfloat16)] * 2
    arrays = [*pieces, shares, *experts[0], *experts[1]]
    inside = pl.BlockSpec(memory_space=pltpu.VMEM)
    return pl.pallas_call(
        functools.partial(expert_kernel, len(pieces), places),
        in_specs=[whole(array.shape) for array in arrays[:-6]] + [inside] * 6,
        out_specs=[whole(result.shape) for result in results],
        grid=(1,),
        out_shape=results,
        compiler_params=pltpu.CompilerParams(vmem_limit_bytes=16 << 20),
    )(*arrays)


def ring_body(
    residual_in,
    queries,
    question_key_values,
    document_prefix_cache,
    out_proj,
    norm_gain,
    routes,
    keep_mask,
    route_weights,
    expert_slots,
    expert_gate,
    expert_up,
    expert_down,
):
    local_tokens = queries.shape[0]
    line = lax.axis_index("line")
    lines = lax.axis_size("line")
    pairs = lines // 2
    last = pairs // 2
    member = line & 1
    other = 1 - member
    offsets = list(range(-last, pairs - last))

    table = []
    for device in range(lines):
        spot = ring_spot(device // 2, pairs)
        held = [ring_pair((spot + offset) % pairs, pairs) for offset in offsets]
        table.append([(pair // last ^ device % 2) * last + pair % last for pair in held])
    places = lax.dynamic_index_in_dim(jnp.array(table, jnp.int32), line, 0, keepdims=False)

    def half(array, which):
        return lax.dynamic_slice_in_dim(
            array, which * (array.shape[1] // 2), array.shape[1] // 2, axis=1
        )

    def both(left, right, which):
        return jnp.concatenate([half(left, which), half(right, which)], axis=1)

    projections = ring_gather(out_proj, True)

    kv_columns = KEY_VALUE_HEADS * HEAD_SIZE
    prefix_keys = document_prefix_cache[:, :kv_columns]
    prefix_values = document_prefix_cache[:, kv_columns:]
    slab = jnp.concatenate(
        [
            both(prefix_keys, prefix_values, member),
            swap(both(prefix_keys, prefix_values, other)),
        ],
        axis=0,
    )
    slots = expert_slots.shape[0]
    pieces = three_parts(slot_weights(routes, keep_mask, route_weights, expert_slots).T)
    pieces.append(jnp.zeros((slots, 2 * HEAD_SIZE - 3 * local_tokens), jnp.bfloat16))
    arrived = ring_gather(jnp.concatenate([slab, jnp.concatenate(pieces, axis=1)], axis=0), False)
    prefix_rows = slab.shape[0]
    wanted = jnp.stack([line, line ^ 1])
    chooser = (jnp.arange(slots, dtype=jnp.int32)[:, None] == wanted[None, :]).astype(jnp.bfloat16)

    mine = (expert_gate[0], expert_up[0], expert_down[0])
    experts = (mine, tuple(swap(array) for array in mine))

    question_keys = question_key_values[:, :kv_columns]
    question_values = question_key_values[:, kv_columns:]
    own_pack = jnp.concatenate(
        [half(queries, member), both(question_keys, question_values, member)], axis=1
    )
    send_pack = jnp.concatenate(
        [half(queries, other), both(question_keys, question_values, other)], axis=1
    )
    kept, sent, all_shares = attention(
        member,
        own_pack,
        swap(send_pack),
        chooser,
        [arrived[o] for o in offsets],
        prefix_rows,
    )

    early = [o for o in offsets if abs(o) < last - 1]
    late = [o for o in offsets if abs(o) >= last - 1]
    batches = [[0, -1, 1]] + [[-step, step] for step in range(2, last)] + [[-last]]
    sent, places = lax.optimization_barrier((sent, places))
    received = swap(sent)
    received, theirs = lax.optimization_barrier((received, experts[1]))

    def projected(batch, starts):
        numbers = tuple(offsets.index(o) for o in batch)
        return project(
            places,
            numbers,
            kept,
            received,
            starts,
            [projections[o] for o in batch],
            offsets.index(-last),
        )

    for_me, for_partner = projected(late, projected(early, []))
    shape = residual_in.shape
    mixture, normed = pl.pallas_call(
        norm_kernel,
        out_shape=[
            jax.ShapeDtypeStruct(shape, jnp.float32),
            jax.ShapeDtypeStruct(shape, jnp.bfloat16),
        ],
        compiler_params=pltpu.CompilerParams(vmem_limit_bytes=8 << 20),
    )(residual_in, for_me, swap(for_partner), norm_gain[None, :])

    rows = ring_gather(normed, False)
    experts = (mine, load(theirs))
    parts = {}
    for batch in batches:
        found = run_experts(
            [rows[o] for o in batch],
            all_shares,
            [offsets.index(o) for o in batch],
            experts,
            batch == [-last],
        )
        if batch == [-last]:
            parts[-last] = tuple(found)
        else:
            parts.update(zip(batch, found))
    return (mixture + ring_sum(parts)).astype(jnp.bfloat16)


def solution(mesh):
    placed = (
        P(("group", "line"), None),
        P(("group", "line"), None),
        P(("group", "line"), None),
        P(("group", "line"), None),
        P("line", None),
        P(),
        P(("group", "line"), None),
        P(("group", "line"), None),
        P(("group", "line"), None),
        P(),
        P("line", None, None),
        P("line", None, None),
        P("line", None, None),
    )

    tokens_of = lambda arrays: arrays[1].shape[0] // mesh.size

    def layer(*arrays):
        tokens, experts = tokens_of(arrays), arrays[9].shape[0]
        dense = 2 * (tokens * TOPK // experts) >= tokens
        ring = dense and mesh.shape["line"] == QUERY_HEADS and experts == mesh.shape["line"]
        return jax.shard_map(
            ring_body if ring else body,
            mesh=mesh,
            in_specs=placed,
            out_specs=P(("group", "line"), None),
            check_vma=False,
        )(*arrays)

    return layer
```

```python
import functools
import math

import jax
import jax.numpy as jnp
import numpy as np
from jax import lax
from jax.experimental import pallas as pl
from jax.experimental.pallas import tpu as pltpu
from jax.sharding import PartitionSpec as P


QUERY_HEADS = 16
KEY_VALUE_HEADS = 2
HEAD_SIZE = 128
TOPK = 8
QLEN = 16


def partner(array, axis, bit):
    return lax.ppermute(array, axis, [(i, i ^ 1 << bit) for i in range(lax.axis_size(axis))])


def shifted(value, axis, steps):
    count = lax.axis_size(axis)
    pairs = [(source, (source + steps) % count) for source in range(count)]
    return lax.ppermute(value, axis, pairs)


def expert_answers(received, expert_gate, expert_up, expert_down):
    buffer_shape = received.shape
    flat_rows = received.reshape(-1, buffer_shape[-1])
    gate_proj = jnp.dot(flat_rows, expert_gate[0], preferred_element_type=jnp.float32)
    upper = jnp.dot(flat_rows, expert_up[0], preferred_element_type=jnp.float32)
    middle = (jax.nn.silu(gate_proj) * upper).astype(jnp.bfloat16)
    return (
        jnp.dot(middle, expert_down[0], preferred_element_type=jnp.float32)
        .astype(jnp.bfloat16)
        .reshape(buffer_shape)
    )


def mix_experts(
    normed_rows,
    route_rows,
    keep_rows,
    weight_rows,
    expert_slots,
    expert_gate,
    expert_up,
    expert_down,
    slot_cap,
):
    row_count = normed_rows.shape[0]
    model_width = normed_rows.shape[1]
    line_count = lax.axis_size("line")
    pair_count = row_count * TOPK
    expert_ids = route_rows.reshape(pair_count)
    kept_pairs = keep_rows.reshape(pair_count) > 0
    numbers = jnp.arange(expert_slots.shape[0], dtype=jnp.int32)
    matches = expert_ids[:, None] == numbers[None, :]
    target = jnp.sum(jnp.where(matches, expert_slots[None, :], 0), axis=1)
    chosen = (matches & kept_pairs[:, None]).astype(jnp.bfloat16)
    pair_order = jnp.arange(pair_count, dtype=jnp.int32)
    earlier = (pair_order[:, None] > pair_order[None, :]).astype(jnp.bfloat16)
    before = jnp.dot(earlier, chosen, preferred_element_type=jnp.float32)
    slot_rank = jnp.sum(before * chosen.astype(jnp.float32), axis=1).astype(jnp.int32)
    slot_index = jnp.where(kept_pairs, target * slot_cap + slot_rank, line_count * slot_cap)
    slot_owner = (
        jnp.full((line_count * slot_cap,), pair_count, jnp.int32)
        .at[slot_index]
        .set(pair_order, mode="drop")
    )
    source_row = jnp.where(slot_owner < pair_count, slot_owner // TOPK, row_count)
    padded = jnp.concatenate([normed_rows, jnp.zeros((1, model_width), jnp.bfloat16)], axis=0)
    buffer = padded[source_row].reshape(line_count, slot_cap, model_width)
    returned = lax.all_to_all(
        expert_answers(
            lax.all_to_all(buffer, "line", split_axis=0, concat_axis=0, tiled=True),
            expert_gate,
            expert_up,
            expert_down,
        ),
        "line",
        split_axis=0,
        concat_axis=0,
        tiled=True,
    )
    padded_back = jnp.concatenate(
        [
            returned.reshape(line_count * slot_cap, model_width),
            jnp.zeros((1, model_width), jnp.bfloat16),
        ],
        axis=0,
    )
    per_pair = padded_back[slot_index].reshape(row_count, TOPK, model_width)
    weight = jnp.where(kept_pairs, weight_rows.reshape(pair_count), 0.0).reshape(row_count, TOPK)
    return jnp.sum(per_pair.astype(jnp.float32) * weight[:, :, None], axis=1)


def near_state(heads_of_queries, local_keys, local_values, score_scale):
    local_tokens = heads_of_queries.shape[0]
    near_scores = (
        jnp.einsum(
            "thgd,shd->thgs", heads_of_queries, local_keys, preferred_element_type=jnp.float32
        )
        * score_scale
    )
    position = jnp.arange(local_tokens, dtype=jnp.int32)
    visible_mask = (position[:, None] // QLEN == position[None, :] // QLEN) & (
        position[None, :] <= position[:, None]
    )
    near_scores = jnp.where(visible_mask[:, None, None, :], near_scores, -1e30)
    run_max = near_scores.max(-1)
    exp_terms = jnp.exp(near_scores - run_max[..., None])
    run_sum = exp_terms.sum(-1)
    run_acc = jnp.einsum(
        "thgs,shd->thgd",
        exp_terms.astype(jnp.bfloat16),
        local_values,
        preferred_element_type=jnp.float32,
    )
    return (run_max, run_sum, run_acc)


def fold_block(carry, piece, heads_of_queries, kv_heads, score_scale):
    old_max, old_sum, old_acc = carry
    piece_rows = piece.shape[0]
    piece_keys = piece[:, : kv_heads * HEAD_SIZE].reshape(piece_rows, kv_heads, HEAD_SIZE)
    piece_vals = piece[:, kv_heads * HEAD_SIZE :].reshape(piece_rows, kv_heads, HEAD_SIZE)
    far_scores = (
        jnp.einsum(
            "thgd,nhd->thgn", heads_of_queries, piece_keys, preferred_element_type=jnp.float32
        )
        * score_scale
    )
    new_max = jnp.maximum(old_max, far_scores.max(-1))
    factor = jnp.exp(old_max - new_max)
    far_terms = jnp.exp(far_scores - new_max[..., None])
    new_acc = old_acc * factor[..., None] + jnp.einsum(
        "thgn,nhd->thgd",
        far_terms.astype(jnp.bfloat16),
        piece_vals,
        preferred_element_type=jnp.float32,
    )
    return (new_max, old_sum * factor + far_terms.sum(-1), new_acc)


def body(
    residual_in,
    queries,
    question_key_values,
    document_prefix_cache,
    out_proj,
    norm_gain,
    routes,
    keep_mask,
    route_weights,
    expert_slots,
    expert_gate,
    expert_up,
    expert_down,
):
    local_tokens = queries.shape[0]
    queries_per_key_head = QUERY_HEADS // KEY_VALUE_HEADS
    score_scale = 1.0 / math.sqrt(HEAD_SIZE)
    half_kv = KEY_VALUE_HEADS // 2
    query_width = half_kv * queries_per_key_head * HEAD_SIZE
    kv_width = half_kv * HEAD_SIZE
    member = lax.axis_index("line") % 2
    other = 1 - member
    query_split = queries.reshape(local_tokens, 2, query_width)
    key_split = question_key_values[:, : KEY_VALUE_HEADS * HEAD_SIZE].reshape(
        local_tokens, 2, kv_width
    )
    value_split = question_key_values[:, KEY_VALUE_HEADS * HEAD_SIZE :].reshape(
        local_tokens, 2, kv_width
    )
    own_pack = jnp.concatenate(
        [
            lax.dynamic_index_in_dim(query_split, member, 1, keepdims=False),
            lax.dynamic_index_in_dim(key_split, member, 1, keepdims=False),
            lax.dynamic_index_in_dim(value_split, member, 1, keepdims=False),
        ],
        axis=1,
    )
    send_pack = jnp.concatenate(
        [
            lax.dynamic_index_in_dim(query_split, other, 1, keepdims=False),
            lax.dynamic_index_in_dim(key_split, other, 1, keepdims=False),
            lax.dynamic_index_in_dim(value_split, other, 1, keepdims=False),
        ],
        axis=1,
    )
    partner_pack = partner(send_pack, "line", 0)
    both_pack = jnp.concatenate([own_pack, partner_pack], axis=0)
    pair_rows = both_pack.shape[0]
    heads_of_queries = both_pack[:, :query_width].reshape(
        pair_rows, half_kv, queries_per_key_head, HEAD_SIZE
    )
    local_keys = both_pack[:, query_width : query_width + kv_width].reshape(
        pair_rows, half_kv, HEAD_SIZE
    )
    local_values = both_pack[:, query_width + kv_width :].reshape(pair_rows, half_kv, HEAD_SIZE)
    start_state = near_state(heads_of_queries, local_keys, local_values, score_scale)
    prefix_rows = document_prefix_cache.shape[0]
    document_keys = document_prefix_cache[:, : KEY_VALUE_HEADS * HEAD_SIZE].reshape(
        prefix_rows, 2, kv_width
    )
    document_values = document_prefix_cache[:, KEY_VALUE_HEADS * HEAD_SIZE :].reshape(
        prefix_rows, 2, kv_width
    )
    own_slab = jnp.concatenate(
        [
            lax.dynamic_index_in_dim(document_keys, member, 1, keepdims=False),
            lax.dynamic_index_in_dim(document_values, member, 1, keepdims=False),
        ],
        axis=1,
    )
    send_slab = jnp.concatenate(
        [
            lax.dynamic_index_in_dim(document_keys, other, 1, keepdims=False),
            lax.dynamic_index_in_dim(document_values, other, 1, keepdims=False),
        ],
        axis=1,
    )
    slab = jnp.concatenate([own_slab, partner(send_slab, "line", 0)], axis=0)
    levels = (lax.axis_size("line") // 2).bit_length() - 1
    for level in range(levels):
        slab = jnp.concatenate([slab, shifted(slab, "line", 2 * (1 << level))], axis=0)
    slab_rows = slab.shape[0]
    block_rows = math.gcd(slab_rows, 2048)
    slab_blocks = slab.reshape(slab_rows // block_rows, block_rows, 2 * kv_width)

    def scan_step(carry, piece):
        return (fold_block(carry, piece, heads_of_queries, half_kv, score_scale), None)

    final_state, _ = lax.scan(scan_step, start_state, slab_blocks)
    _, run_sum, run_acc = final_state
    pair_context = (
        (run_acc / run_sum[..., None]).reshape(pair_rows, query_width).astype(jnp.bfloat16)
    )
    mine = pair_context[:local_tokens]
    returned_context = partner(pair_context[local_tokens:], "line", 0)
    context_rows = jnp.where(
        member == 0,
        jnp.concatenate([mine, returned_context], axis=1),
        jnp.concatenate([returned_context, mine], axis=1),
    )
    attended = jnp.dot(
        context_rows,
        lax.all_gather(out_proj, "line", axis=0, tiled=True),
        preferred_element_type=jnp.float32,
    )
    mixture = residual_in.astype(jnp.float32) + attended
    normed = (
        mixture * lax.rsqrt(jnp.mean(mixture * mixture, axis=-1, keepdims=True) + 1e-06) * norm_gain
    ).astype(jnp.bfloat16)
    half_cap = local_tokens * TOPK // expert_slots.shape[0]
    expert_sum = mix_experts(
        normed,
        routes,
        keep_mask,
        route_weights,
        expert_slots,
        expert_gate,
        expert_up,
        expert_down,
        2 * half_cap,
    )
    return (mixture + expert_sum).astype(jnp.bfloat16)


def ring_spot(pair, pairs):
    row, column = divmod(pair, 2)
    return row if column == 0 else pairs - 1 - row


def ring_pair(spot, pairs):
    return 2 * spot if spot < pairs // 2 else 2 * (pairs - 1 - spot) + 1


def around(value, steps):
    count = lax.axis_size("line")
    pairs = count // 2
    moves = [
        (i, 2 * ring_pair((ring_spot(i // 2, pairs) + steps) % pairs, pairs) + i % 2)
        for i in range(count)
    ]
    return lax.ppermute(value, "line", moves)


def swap(value):
    return partner(value, "line", 0)


def ring_gather(value, last_back=False):
    last = lax.axis_size("line") // 4
    found = {0: value}
    for step in range(1, last):
        found[-step] = around(found[1 - step], 1)
        found[step] = around(found[step - 1], -1)
    if last_back:
        found[-last] = around(found[last - 1], -1)
    else:
        found[-last] = around(found[1 - last], 1)
    return found


def ring_sum(parts):
    pairs = len(parts)
    last = pairs // 2
    first_half, second_half = parts[-last]
    cut = first_half.shape[0]
    forward = around(first_half.astype(jnp.bfloat16), 1).astype(jnp.float32)
    backward = around(second_half.astype(jnp.bfloat16), -1).astype(jnp.float32)
    for step in range(2, last + 1):
        ahead = parts[last + 1 - step]
        behind = parts[step - last - 1]
        if step == 2:
            forward = jnp.concatenate([ahead[:cut] + forward, ahead[cut:]], axis=0)
            backward = jnp.concatenate([behind[:cut], behind[cut:] + backward], axis=0)
        else:
            forward = ahead + forward
            backward = behind + backward
        forward = around(forward.astype(jnp.bfloat16), 1).astype(jnp.float32)
        backward = around(backward.astype(jnp.bfloat16), -1).astype(jnp.float32)
    return parts[0] + forward + backward


def slot_weights(route_rows, keep_rows, weight_rows, expert_slots):
    numbers = jnp.arange(expert_slots.shape[0], dtype=jnp.int32)
    target = jnp.sum(
        jnp.where(route_rows[:, :, None] == numbers, expert_slots[None, None, :], 0), axis=2
    )
    kept = jnp.where(keep_rows > 0, weight_rows, 0.0)
    return jnp.sum(jnp.where(target[:, :, None] == numbers, kept[:, :, None], 0.0), axis=1)


def three_parts(values):
    high = lax.reduce_precision(values, 8, 7)
    rest = values - high
    middle = lax.reduce_precision(rest, 8, 7)
    return [part.astype(jnp.bfloat16) for part in (high, middle, rest - middle)]


def whole(shape):
    return pl.BlockSpec(shape, lambda *_: (0,) * len(shape))


def attention_kernel(member_ref, *refs):
    own_ref, partner_ref = refs[:2]
    prefix_refs, (kept_ref, sent_ref, keys, values) = refs[2:-4], refs[-4:]
    tokens = own_ref.shape[0]
    rows = 2 * tokens
    scale = 1.0 / math.sqrt(HEAD_SIZE)
    query_width = own_ref.shape[1] - 2 * HEAD_SIZE
    contract_last = (((1,), (1,)), ((), ()))

    held = prefix_refs[0].shape[0]
    key_at = pl.multiple_of(member_ref[0] * HEAD_SIZE, HEAD_SIZE)
    value_at = pl.multiple_of((KEY_VALUE_HEADS + member_ref[0]) * HEAD_SIZE, HEAD_SIZE)
    for number, prefix_ref in enumerate(prefix_refs):
        inside = slice(number * held, (number + 1) * held)
        keys[inside, :] = prefix_ref[:, pl.ds(key_at, HEAD_SIZE)]
        values[inside, :] = prefix_ref[:, pl.ds(value_at, HEAD_SIZE)]

    def columns(start):
        at = pl.ds(start, HEAD_SIZE)
        return jnp.concatenate([own_ref[:, at], partner_ref[:, at]], axis=0)

    near_keys = columns(query_width)
    near_values = columns(query_width + HEAD_SIZE)
    row = lax.rem(lax.broadcasted_iota(jnp.int32, (2 * rows, rows), 0), rows)
    column = lax.broadcasted_iota(jnp.int32, (2 * rows, rows), 1)
    visible = (lax.div(row, QLEN) == lax.div(column, QLEN)) & (column <= row)

    def two_heads(number, carry):
        start = pl.multiple_of(2 * number * HEAD_SIZE, 2 * HEAD_SIZE)
        query = jnp.concatenate([columns(start), columns(start + HEAD_SIZE)], axis=0)
        near = lax.dot_general(query, near_keys, contract_last, preferred_element_type=jnp.float32)
        near = jnp.where(visible, near * scale, -1e30)
        far = lax.dot_general(query, keys[...], contract_last, preferred_element_type=jnp.float32)
        far = far * scale
        largest = jnp.maximum(near.max(axis=1, keepdims=True), far.max(axis=1, keepdims=True))
        near_terms, far_terms = jnp.exp(near - largest), jnp.exp(far - largest)
        total = near_terms.sum(axis=1, keepdims=True) + far_terms.sum(axis=1, keepdims=True)
        summed = jnp.dot(
            far_terms.astype(jnp.bfloat16), values[...], preferred_element_type=jnp.float32
        ) + jnp.dot(
            near_terms.astype(jnp.bfloat16), near_values, preferred_element_type=jnp.float32
        )
        result = (summed / total).astype(jnp.bfloat16)
        even, odd = result[:rows], result[rows:]
        first = member_ref[0] == 0
        kept_ref[number] = jnp.where(first, even, odd)
        sent = jnp.where(first, odd, even)
        sent_ref[number] = jnp.concatenate([sent[tokens:], sent[:tokens]], axis=0)
        return carry

    lax.fori_loop(0, query_width // HEAD_SIZE // 2, two_heads, 0)


def attention(member, own_pack, partner_pack, prefix):
    tokens, width = own_pack.shape
    half_heads = (width // HEAD_SIZE - 2) // 2
    shape = (half_heads, 2 * tokens, HEAD_SIZE)
    arrays = [own_pack, partner_pack, *prefix]
    return pl.pallas_call(
        attention_kernel,
        grid_spec=pltpu.PrefetchScalarGridSpec(
            num_scalar_prefetch=1,
            grid=(1,),
            in_specs=[whole(array.shape) for array in arrays],
            out_specs=[whole(shape)] * 2,
            scratch_shapes=[pltpu.VMEM((len(prefix) * prefix[0].shape[0], HEAD_SIZE), jnp.bfloat16)]
            * 2,
        ),
        out_shape=[jax.ShapeDtypeStruct(shape, jnp.bfloat16)] * 2,
    )(member[None], *arrays)


def project_kernel(numbers, carried, place_ref, kept_ref, received_ref, *refs):
    start_refs = refs[: 2 * carried]
    weight_refs = refs[2 * carried : -2]
    out_refs = refs[-2:]
    half_heads = kept_ref.shape[0]
    tokens = out_refs[0].shape[0]
    total = None
    for at, number in enumerate(numbers):
        place = place_ref[number]
        inside = lax.rem(place, half_heads)
        rows = jnp.where(place < half_heads, kept_ref[inside], received_ref[inside])
        weights = jnp.concatenate(
            [weight_refs[2 * at][...], weight_refs[2 * at + 1][...]], axis=0
        )
        product = jnp.dot(rows, weights, preferred_element_type=jnp.float32)
        total = product if total is None else total + product
    for place, out_ref in enumerate(out_refs):
        piece = total[place * tokens : (place + 1) * tokens]
        out_ref[...] = piece + start_refs[place][...] if carried else piece


def project(places, numbers, kept, received, starts, weights):
    shape = (kept.shape[1] // 2, weights[0].shape[1])
    arrays = [kept, received, *starts, *weights]
    return pl.pallas_call(
        functools.partial(project_kernel, numbers, bool(starts)),
        grid_spec=pltpu.PrefetchScalarGridSpec(
            num_scalar_prefetch=1,
            grid=(1,),
            in_specs=[whole(array.shape) for array in arrays],
            out_specs=[whole(shape)] * 2,
        ),
        out_shape=[jax.ShapeDtypeStruct(shape, jnp.float32)] * 2,
        compiler_params=pltpu.CompilerParams(vmem_limit_bytes=16 << 20),
    )(places, *arrays)


def norm_kernel(residual_ref, mine_ref, theirs_ref, gain_ref, share_ref, mixture_ref, sent_ref):
    mixture = residual_ref[...].astype(jnp.float32) + mine_ref[...] + theirs_ref[...]
    mixture_ref[...] = mixture
    mean = jnp.mean(mixture * mixture, axis=-1, keepdims=True)
    normed = (mixture * lax.rsqrt(mean + 1e-06) * gain_ref[...]).astype(jnp.bfloat16)
    sent_ref[...] = jnp.concatenate([normed, share_ref[...]], axis=1)


def expert_kernel(count, *refs):
    row_refs, chooser_ref, weight_refs, out_refs = (
        refs[:count],
        refs[count],
        refs[count + 1 : count + 7],
        refs[count + 7 :],
    )
    width = 2 * out_refs[0].shape[1]
    rows = jnp.concatenate([row_ref[:, :width] for row_ref in row_refs], axis=0)
    parts = jnp.concatenate([row_ref[:, width:] for row_ref in row_refs], axis=0)
    shares = jnp.dot(parts, chooser_ref[...], preferred_element_type=jnp.float32)
    hidden = weight_refs[0].shape[1]
    tile = 256 if hidden % 256 == 0 else hidden
    result = None
    for number in range(2):
        gate_ref, up_ref, down_ref = weight_refs[3 * number : 3 * number + 3]
        answer = None
        for begin in range(0, hidden, tile):
            inside = slice(begin, begin + tile)
            gate = jnp.dot(rows, gate_ref[:, inside], preferred_element_type=jnp.float32)
            upper = jnp.dot(rows, up_ref[:, inside], preferred_element_type=jnp.float32)
            middle = (gate / (1.0 + jnp.exp(-gate)) * upper).astype(jnp.bfloat16)
            piece = jnp.dot(middle, down_ref[inside, :], preferred_element_type=jnp.float32)
            answer = piece if answer is None else answer + piece
        rounded = answer.astype(jnp.bfloat16).astype(jnp.float32)
        weighted = rounded * shares[:, number : number + 1]
        result = weighted if result is None else result + weighted
    begin = 0
    for left_ref, right_ref in zip(out_refs[0::2], out_refs[1::2]):
        piece = result[begin : begin + left_ref.shape[0]]
        begin += left_ref.shape[0]
        left_ref[...] = piece[:, : width // 2].astype(left_ref.dtype)
        right_ref[...] = piece[:, width // 2 :].astype(right_ref.dtype)


def load_kernel(*refs):
    count = len(refs) // 2
    copies = [
        pltpu.make_async_copy(refs[n], refs[count + n], refs[2 * count].at[n])
        for n in range(count)
    ]
    for copy in copies:
        copy.start()
    for copy in copies:
        copy.wait()


def load(arrays):
    return pl.pallas_call(
        load_kernel,
        in_specs=[pl.BlockSpec(memory_space=pl.ANY)] * len(arrays),
        out_specs=[pl.BlockSpec(memory_space=pltpu.VMEM)] * len(arrays),
        out_shape=[jax.ShapeDtypeStruct(array.shape, array.dtype) for array in arrays],
        scratch_shapes=[pltpu.SemaphoreType.DMA((len(arrays),))],
        compiler_params=pltpu.CompilerParams(vmem_limit_bytes=24 << 20),
    )(*arrays)


def run_experts(pieces, chooser, experts, split):
    shape = (pieces[0].shape[0], experts[0][0].shape[0] // 2)
    results = [jax.ShapeDtypeStruct(shape, jnp.float32)] * (2 * len(pieces))
    if split:
        halved = (shape[0] // 2, shape[1])
        results[:2] = [jax.ShapeDtypeStruct(halved, jnp.bfloat16)] * 4
    arrays = [*pieces, chooser, *experts[0], *experts[1]]
    inside = pl.BlockSpec(memory_space=pltpu.VMEM)
    return pl.pallas_call(
        functools.partial(expert_kernel, len(pieces)),
        in_specs=[whole(array.shape) for array in arrays[:-6]] + [inside] * 6,
        out_specs=[whole(result.shape) for result in results],
        grid=(1,),
        out_shape=results,
        compiler_params=pltpu.CompilerParams(vmem_limit_bytes=16 << 20),
    )(*arrays)


def ring_body(
    residual_in,
    queries,
    question_key_values,
    document_prefix_cache,
    out_proj,
    norm_gain,
    routes,
    keep_mask,
    route_weights,
    expert_slots,
    expert_gate,
    expert_up,
    expert_down,
):
    local_tokens = queries.shape[0]
    line = lax.axis_index("line")
    lines = lax.axis_size("line")
    pairs = lines // 2
    last = pairs // 2
    member = line & 1
    other = 1 - member
    offsets = list(range(-last, pairs - last))

    table = []
    for device in range(lines):
        spot = ring_spot(device // 2, pairs)
        held = [ring_pair((spot + offset) % pairs, pairs) for offset in offsets]
        table.append([(pair // last ^ device % 2) * last + pair % last for pair in held])
    places = lax.dynamic_index_in_dim(jnp.array(table, jnp.int32), line, 0, keepdims=False)

    def half(array, which):
        return lax.dynamic_slice_in_dim(
            array, which * (array.shape[1] // 2), array.shape[1] // 2, axis=1
        )

    def both(left, right, which):
        return jnp.concatenate([half(left, which), half(right, which)], axis=1)

    arrived = ring_gather(document_prefix_cache)
    prefix = []
    for offset in offsets:
        prefix += [arrived[offset], swap(arrived[offset])]
    cut = out_proj.shape[0] // 2
    upper_rows = ring_gather(out_proj[:cut])
    lower_rows = ring_gather(out_proj[cut:], True)

    slots = expert_slots.shape[0]
    lanes = -(-3 * slots // HEAD_SIZE) * HEAD_SIZE
    pieces = three_parts(slot_weights(routes, keep_mask, route_weights, expert_slots))
    pieces.append(jnp.zeros((local_tokens, lanes - 3 * slots), jnp.bfloat16))
    slot_parts = jnp.concatenate(pieces, axis=1)
    lane = np.arange(lanes)
    slot_of_lane = jnp.array(np.where(lane < 3 * slots, lane % slots, -1), jnp.int32)
    wanted = jnp.stack([line, line ^ 1])
    chooser = (slot_of_lane[:, None] == wanted[None, :]).astype(jnp.bfloat16)

    mine = (expert_gate[0], expert_up[0], expert_down[0])
    experts = (mine, tuple(swap(array) for array in mine))

    kv_columns = KEY_VALUE_HEADS * HEAD_SIZE
    question_keys = question_key_values[:, :kv_columns]
    question_values = question_key_values[:, kv_columns:]
    own_pack = jnp.concatenate(
        [half(queries, member), both(question_keys, question_values, member)], axis=1
    )
    send_pack = jnp.concatenate(
        [half(queries, other), both(question_keys, question_values, other)], axis=1
    )
    own_pack, send_pack, places, slot_parts, chooser = lax.optimization_barrier(
        (own_pack, send_pack, places, slot_parts, chooser)
    )
    kept, sent = attention(member, own_pack, swap(send_pack), prefix)

    early = [o for o in offsets if abs(o) < last - 1]
    late = [o for o in offsets if abs(o) >= last - 1]
    batches = [[0, -1, 1]] + [[-step, step] for step in range(2, last)] + [[-last]]
    received = swap(sent)
    received, theirs = lax.optimization_barrier((received, experts[1]))

    def projected(batch, starts):
        numbers = tuple(offsets.index(o) for o in batch)
        return project(
            places,
            numbers,
            kept,
            received,
            starts,
            [array[o] for o in batch for array in (upper_rows, lower_rows)],
        )

    for_me, for_partner = projected(late, projected(early, []))
    shape = residual_in.shape
    mixture, normed = pl.pallas_call(
        norm_kernel,
        out_shape=[
            jax.ShapeDtypeStruct(shape, jnp.float32),
            jax.ShapeDtypeStruct((shape[0], shape[1] + lanes), jnp.bfloat16),
        ],
        compiler_params=pltpu.CompilerParams(vmem_limit_bytes=8 << 20),
    )(residual_in, for_me, swap(for_partner), norm_gain[None, :], slot_parts)

    rows = ring_gather(normed)
    held = load([*mine, *theirs])
    experts = (held[:3], held[3:])
    left, right = {}, {}
    for batch in batches:
        found = run_experts([rows[o] for o in batch], chooser, experts, batch == [-last])
        for parts, pieces in ((left, found[0::2]), (right, found[1::2])):
            if batch == [-last]:
                parts[-last] = tuple(pieces)
            else:
                parts.update(zip(batch, pieces))
    expert_sum = jnp.concatenate([ring_sum(left), ring_sum(right)], axis=1)
    return (mixture + expert_sum).astype(jnp.bfloat16)


def solution(mesh):
    placed = (
        P(("group", "line"), None),
        P(("group", "line"), None),
        P(("group", "line"), None),
        P(("group", "line"), None),
        P("line", None),
        P(),
        P(("group", "line"), None),
        P(("group", "line"), None),
        P(("group", "line"), None),
        P(),
        P("line", None, None),
        P("line", None, None),
        P("line", None, None),
    )

    tokens_of = lambda arrays: arrays[1].shape[0] // mesh.size

    def layer(*arrays):
        tokens, experts = tokens_of(arrays), arrays[9].shape[0]
        dense = 2 * (tokens * TOPK // experts) >= tokens
        ring = dense and mesh.shape["line"] == QUERY_HEADS and experts == mesh.shape["line"]
        return jax.shard_map(
            ring_body if ring else body,
            mesh=mesh,
            in_specs=placed,
            out_specs=P(("group", "line"), None),
            check_vma=False,
        )(*arrays)

    return layer
```

```python
import functools
import math

import jax
import jax.numpy as jnp
import numpy as np
from jax import lax
from jax.experimental import pallas as pl
from jax.experimental.pallas import tpu as pltpu
from jax.sharding import PartitionSpec as P


QUERY_HEADS = 16
KEY_VALUE_HEADS = 2
HEAD_SIZE = 128
TOPK = 8
QLEN = 16


def partner(array, axis, bit):
    return lax.ppermute(array, axis, [(i, i ^ 1 << bit) for i in range(lax.axis_size(axis))])


def shifted(value, axis, steps):
    count = lax.axis_size(axis)
    pairs = [(source, (source + steps) % count) for source in range(count)]
    return lax.ppermute(value, axis, pairs)


def expert_answers(received, expert_gate, expert_up, expert_down):
    buffer_shape = received.shape
    flat_rows = received.reshape(-1, buffer_shape[-1])
    gate_proj = jnp.dot(flat_rows, expert_gate[0], preferred_element_type=jnp.float32)
    upper = jnp.dot(flat_rows, expert_up[0], preferred_element_type=jnp.float32)
    middle = (jax.nn.silu(gate_proj) * upper).astype(jnp.bfloat16)
    return (
        jnp.dot(middle, expert_down[0], preferred_element_type=jnp.float32)
        .astype(jnp.bfloat16)
        .reshape(buffer_shape)
    )


def mix_experts(
    normed_rows,
    route_rows,
    keep_rows,
    weight_rows,
    expert_slots,
    expert_gate,
    expert_up,
    expert_down,
    slot_cap,
):
    row_count = normed_rows.shape[0]
    model_width = normed_rows.shape[1]
    line_count = lax.axis_size("line")
    pair_count = row_count * TOPK
    expert_ids = route_rows.reshape(pair_count)
    kept_pairs = keep_rows.reshape(pair_count) > 0
    numbers = jnp.arange(expert_slots.shape[0], dtype=jnp.int32)
    matches = expert_ids[:, None] == numbers[None, :]
    target = jnp.sum(jnp.where(matches, expert_slots[None, :], 0), axis=1)
    chosen = (matches & kept_pairs[:, None]).astype(jnp.bfloat16)
    pair_order = jnp.arange(pair_count, dtype=jnp.int32)
    earlier = (pair_order[:, None] > pair_order[None, :]).astype(jnp.bfloat16)
    before = jnp.dot(earlier, chosen, preferred_element_type=jnp.float32)
    slot_rank = jnp.sum(before * chosen.astype(jnp.float32), axis=1).astype(jnp.int32)
    slot_index = jnp.where(kept_pairs, target * slot_cap + slot_rank, line_count * slot_cap)
    slot_owner = (
        jnp.full((line_count * slot_cap,), pair_count, jnp.int32)
        .at[slot_index]
        .set(pair_order, mode="drop")
    )
    source_row = jnp.where(slot_owner < pair_count, slot_owner // TOPK, row_count)
    padded = jnp.concatenate([normed_rows, jnp.zeros((1, model_width), jnp.bfloat16)], axis=0)
    buffer = padded[source_row].reshape(line_count, slot_cap, model_width)
    returned = lax.all_to_all(
        expert_answers(
            lax.all_to_all(buffer, "line", split_axis=0, concat_axis=0, tiled=True),
            expert_gate,
            expert_up,
            expert_down,
        ),
        "line",
        split_axis=0,
        concat_axis=0,
        tiled=True,
    )
    padded_back = jnp.concatenate(
        [
            returned.reshape(line_count * slot_cap, model_width),
            jnp.zeros((1, model_width), jnp.bfloat16),
        ],
        axis=0,
    )
    per_pair = padded_back[slot_index].reshape(row_count, TOPK, model_width)
    weight = jnp.where(kept_pairs, weight_rows.reshape(pair_count), 0.0).reshape(row_count, TOPK)
    return jnp.sum(per_pair.astype(jnp.float32) * weight[:, :, None], axis=1)


def near_state(heads_of_queries, local_keys, local_values, score_scale):
    local_tokens = heads_of_queries.shape[0]
    near_scores = (
        jnp.einsum(
            "thgd,shd->thgs", heads_of_queries, local_keys, preferred_element_type=jnp.float32
        )
        * score_scale
    )
    position = jnp.arange(local_tokens, dtype=jnp.int32)
    visible_mask = (position[:, None] // QLEN == position[None, :] // QLEN) & (
        position[None, :] <= position[:, None]
    )
    near_scores = jnp.where(visible_mask[:, None, None, :], near_scores, -1e30)
    run_max = near_scores.max(-1)
    exp_terms = jnp.exp(near_scores - run_max[..., None])
    run_sum = exp_terms.sum(-1)
    run_acc = jnp.einsum(
        "thgs,shd->thgd",
        exp_terms.astype(jnp.bfloat16),
        local_values,
        preferred_element_type=jnp.float32,
    )
    return (run_max, run_sum, run_acc)


def fold_block(carry, piece, heads_of_queries, kv_heads, score_scale):
    old_max, old_sum, old_acc = carry
    piece_rows = piece.shape[0]
    piece_keys = piece[:, : kv_heads * HEAD_SIZE].reshape(piece_rows, kv_heads, HEAD_SIZE)
    piece_vals = piece[:, kv_heads * HEAD_SIZE :].reshape(piece_rows, kv_heads, HEAD_SIZE)
    far_scores = (
        jnp.einsum(
            "thgd,nhd->thgn", heads_of_queries, piece_keys, preferred_element_type=jnp.float32
        )
        * score_scale
    )
    new_max = jnp.maximum(old_max, far_scores.max(-1))
    factor = jnp.exp(old_max - new_max)
    far_terms = jnp.exp(far_scores - new_max[..., None])
    new_acc = old_acc * factor[..., None] + jnp.einsum(
        "thgn,nhd->thgd",
        far_terms.astype(jnp.bfloat16),
        piece_vals,
        preferred_element_type=jnp.float32,
    )
    return (new_max, old_sum * factor + far_terms.sum(-1), new_acc)


def body(
    residual_in,
    queries,
    question_key_values,
    document_prefix_cache,
    out_proj,
    norm_gain,
    routes,
    keep_mask,
    route_weights,
    expert_slots,
    expert_gate,
    expert_up,
    expert_down,
):
    local_tokens = queries.shape[0]
    queries_per_key_head = QUERY_HEADS // KEY_VALUE_HEADS
    score_scale = 1.0 / math.sqrt(HEAD_SIZE)
    half_kv = KEY_VALUE_HEADS // 2
    query_width = half_kv * queries_per_key_head * HEAD_SIZE
    kv_width = half_kv * HEAD_SIZE
    member = lax.axis_index("line") % 2
    other = 1 - member
    query_split = queries.reshape(local_tokens, 2, query_width)
    key_split = question_key_values[:, : KEY_VALUE_HEADS * HEAD_SIZE].reshape(
        local_tokens, 2, kv_width
    )
    value_split = question_key_values[:, KEY_VALUE_HEADS * HEAD_SIZE :].reshape(
        local_tokens, 2, kv_width
    )
    own_pack = jnp.concatenate(
        [
            lax.dynamic_index_in_dim(query_split, member, 1, keepdims=False),
            lax.dynamic_index_in_dim(key_split, member, 1, keepdims=False),
            lax.dynamic_index_in_dim(value_split, member, 1, keepdims=False),
        ],
        axis=1,
    )
    send_pack = jnp.concatenate(
        [
            lax.dynamic_index_in_dim(query_split, other, 1, keepdims=False),
            lax.dynamic_index_in_dim(key_split, other, 1, keepdims=False),
            lax.dynamic_index_in_dim(value_split, other, 1, keepdims=False),
        ],
        axis=1,
    )
    partner_pack = partner(send_pack, "line", 0)
    both_pack = jnp.concatenate([own_pack, partner_pack], axis=0)
    pair_rows = both_pack.shape[0]
    heads_of_queries = both_pack[:, :query_width].reshape(
        pair_rows, half_kv, queries_per_key_head, HEAD_SIZE
    )
    local_keys = both_pack[:, query_width : query_width + kv_width].reshape(
        pair_rows, half_kv, HEAD_SIZE
    )
    local_values = both_pack[:, query_width + kv_width :].reshape(pair_rows, half_kv, HEAD_SIZE)
    start_state = near_state(heads_of_queries, local_keys, local_values, score_scale)
    prefix_rows = document_prefix_cache.shape[0]
    document_keys = document_prefix_cache[:, : KEY_VALUE_HEADS * HEAD_SIZE].reshape(
        prefix_rows, 2, kv_width
    )
    document_values = document_prefix_cache[:, KEY_VALUE_HEADS * HEAD_SIZE :].reshape(
        prefix_rows, 2, kv_width
    )
    own_slab = jnp.concatenate(
        [
            lax.dynamic_index_in_dim(document_keys, member, 1, keepdims=False),
            lax.dynamic_index_in_dim(document_values, member, 1, keepdims=False),
        ],
        axis=1,
    )
    send_slab = jnp.concatenate(
        [
            lax.dynamic_index_in_dim(document_keys, other, 1, keepdims=False),
            lax.dynamic_index_in_dim(document_values, other, 1, keepdims=False),
        ],
        axis=1,
    )
    slab = jnp.concatenate([own_slab, partner(send_slab, "line", 0)], axis=0)
    levels = (lax.axis_size("line") // 2).bit_length() - 1
    for level in range(levels):
        slab = jnp.concatenate([slab, shifted(slab, "line", 2 * (1 << level))], axis=0)
    slab_rows = slab.shape[0]
    block_rows = math.gcd(slab_rows, 2048)
    slab_blocks = slab.reshape(slab_rows // block_rows, block_rows, 2 * kv_width)

    def scan_step(carry, piece):
        return (fold_block(carry, piece, heads_of_queries, half_kv, score_scale), None)

    final_state, _ = lax.scan(scan_step, start_state, slab_blocks)
    _, run_sum, run_acc = final_state
    pair_context = (
        (run_acc / run_sum[..., None]).reshape(pair_rows, query_width).astype(jnp.bfloat16)
    )
    mine = pair_context[:local_tokens]
    returned_context = partner(pair_context[local_tokens:], "line", 0)
    context_rows = jnp.where(
        member == 0,
        jnp.concatenate([mine, returned_context], axis=1),
        jnp.concatenate([returned_context, mine], axis=1),
    )
    attended = jnp.dot(
        context_rows,
        lax.all_gather(out_proj, "line", axis=0, tiled=True),
        preferred_element_type=jnp.float32,
    )
    mixture = residual_in.astype(jnp.float32) + attended
    normed = (
        mixture * lax.rsqrt(jnp.mean(mixture * mixture, axis=-1, keepdims=True) + 1e-06) * norm_gain
    ).astype(jnp.bfloat16)
    half_cap = local_tokens * TOPK // expert_slots.shape[0]
    expert_sum = mix_experts(
        normed,
        routes,
        keep_mask,
        route_weights,
        expert_slots,
        expert_gate,
        expert_up,
        expert_down,
        2 * half_cap,
    )
    return (mixture + expert_sum).astype(jnp.bfloat16)


def ring_spot(pair, pairs):
    row, column = divmod(pair, 2)
    return row if column == 0 else pairs - 1 - row


def ring_pair(spot, pairs):
    return 2 * spot if spot < pairs // 2 else 2 * (pairs - 1 - spot) + 1


def around(value, steps):
    count = lax.axis_size("line")
    pairs = count // 2
    moves = [
        (i, 2 * ring_pair((ring_spot(i // 2, pairs) + steps) % pairs, pairs) + i % 2)
        for i in range(count)
    ]
    return lax.ppermute(value, "line", moves)


def swap(value):
    return partner(value, "line", 0)


def ring_gather(value, last_back=False):
    last = lax.axis_size("line") // 4
    found = {0: value}
    for step in range(1, last):
        found[-step] = around(found[1 - step], 1)
        found[step] = around(found[step - 1], -1)
    if last_back:
        found[-last] = around(found[last - 1], -1)
    else:
        found[-last] = around(found[1 - last], 1)
    return found


def ring_sum(parts):
    pairs = len(parts)
    last = pairs // 2
    first_half, second_half = parts[-last]
    cut = first_half.shape[0]
    forward = around(first_half.astype(jnp.bfloat16), 1).astype(jnp.float32)
    backward = around(second_half.astype(jnp.bfloat16), -1).astype(jnp.float32)
    for step in range(2, last + 1):
        ahead = parts[last + 1 - step]
        behind = parts[step - last - 1]
        if step == 2:
            forward = jnp.concatenate([ahead[:cut] + forward, ahead[cut:]], axis=0)
            backward = jnp.concatenate([behind[:cut], behind[cut:] + backward], axis=0)
        else:
            forward = ahead + forward
            backward = behind + backward
        forward = around(forward.astype(jnp.bfloat16), 1).astype(jnp.float32)
        backward = around(backward.astype(jnp.bfloat16), -1).astype(jnp.float32)
    return parts[0] + forward + backward


def slot_weights(route_rows, keep_rows, weight_rows, expert_slots):
    numbers = jnp.arange(expert_slots.shape[0], dtype=jnp.int32)
    target = jnp.sum(
        jnp.where(route_rows[:, :, None] == numbers, expert_slots[None, None, :], 0), axis=2
    )
    kept = jnp.where(keep_rows > 0, weight_rows, 0.0)
    return jnp.sum(jnp.where(target[:, :, None] == numbers, kept[:, :, None], 0.0), axis=1)


def three_parts(values):
    high = lax.reduce_precision(values, 8, 7)
    rest = values - high
    middle = lax.reduce_precision(rest, 8, 7)
    return [part.astype(jnp.bfloat16) for part in (high, middle, rest - middle)]


def whole(shape):
    return pl.BlockSpec(shape, lambda *_: (0,) * len(shape))


def attention_kernel(member_ref, *refs):
    own_ref, partner_ref = refs[:2]
    prefix_refs, (kept_ref, sent_ref, keys, values) = refs[2:-4], refs[-4:]
    tokens = own_ref.shape[0]
    rows = 2 * tokens
    scale = 1.0 / math.sqrt(HEAD_SIZE)
    query_width = own_ref.shape[1] - 2 * HEAD_SIZE
    contract_last = (((1,), (1,)), ((), ()))

    held = prefix_refs[0].shape[0]
    key_at = pl.multiple_of(member_ref[0] * HEAD_SIZE, HEAD_SIZE)
    value_at = pl.multiple_of((KEY_VALUE_HEADS + member_ref[0]) * HEAD_SIZE, HEAD_SIZE)
    for number, prefix_ref in enumerate(prefix_refs):
        inside = slice(number * held, (number + 1) * held)
        keys[inside, :] = prefix_ref[:, pl.ds(key_at, HEAD_SIZE)]
        values[inside, :] = prefix_ref[:, pl.ds(value_at, HEAD_SIZE)]

    def columns(start):
        at = pl.ds(start, HEAD_SIZE)
        return jnp.concatenate([own_ref[:, at], partner_ref[:, at]], axis=0)

    near_keys = columns(query_width)
    near_values = columns(query_width + HEAD_SIZE)
    row = lax.rem(lax.broadcasted_iota(jnp.int32, (2 * rows, rows), 0), rows)
    column = lax.broadcasted_iota(jnp.int32, (2 * rows, rows), 1)
    visible = (lax.div(row, QLEN) == lax.div(column, QLEN)) & (column <= row)

    def two_heads(number, carry):
        start = pl.multiple_of(2 * number * HEAD_SIZE, 2 * HEAD_SIZE)
        query = jnp.concatenate([columns(start), columns(start + HEAD_SIZE)], axis=0)
        near = lax.dot_general(query, near_keys, contract_last, preferred_element_type=jnp.float32)
        near = jnp.where(visible, near * scale, -1e30)
        far = lax.dot_general(query, keys[...], contract_last, preferred_element_type=jnp.float32)
        far = far * scale
        largest = jnp.maximum(near.max(axis=1, keepdims=True), far.max(axis=1, keepdims=True))
        near_terms, far_terms = jnp.exp(near - largest), jnp.exp(far - largest)
        total = near_terms.sum(axis=1, keepdims=True) + far_terms.sum(axis=1, keepdims=True)
        summed = jnp.dot(
            far_terms.astype(jnp.bfloat16), values[...], preferred_element_type=jnp.float32
        ) + jnp.dot(
            near_terms.astype(jnp.bfloat16), near_values, preferred_element_type=jnp.float32
        )
        result = (summed / total).astype(jnp.bfloat16)
        even, odd = result[:rows], result[rows:]
        first = member_ref[0] == 0
        kept_ref[number] = jnp.where(first, even, odd)
        sent = jnp.where(first, odd, even)
        sent_ref[number] = jnp.concatenate([sent[tokens:], sent[:tokens]], axis=0)
        return carry

    lax.fori_loop(0, query_width // HEAD_SIZE // 2, two_heads, 0)


def attention(member, own_pack, partner_pack, prefix):
    tokens, width = own_pack.shape
    half_heads = (width // HEAD_SIZE - 2) // 2
    shape = (half_heads, 2 * tokens, HEAD_SIZE)
    arrays = [own_pack, partner_pack, *prefix]
    return pl.pallas_call(
        attention_kernel,
        grid_spec=pltpu.PrefetchScalarGridSpec(
            num_scalar_prefetch=1,
            grid=(1,),
            in_specs=[whole(array.shape) for array in arrays],
            out_specs=[whole(shape)] * 2,
            scratch_shapes=[pltpu.VMEM((len(prefix) * prefix[0].shape[0], HEAD_SIZE), jnp.bfloat16)]
            * 2,
        ),
        out_shape=[jax.ShapeDtypeStruct(shape, jnp.bfloat16)] * 2,
        compiler_params=pltpu.CompilerParams(vmem_limit_bytes=24 << 20),
    )(member[None], *arrays)


def project_kernel(numbers, carried, place_ref, kept_ref, received_ref, *refs):
    start_refs = refs[: 2 * carried]
    weight_refs = refs[2 * carried : -2]
    out_refs = refs[-2:]
    half_heads = kept_ref.shape[0]
    tokens = out_refs[0].shape[0]
    total = None
    for at, number in enumerate(numbers):
        place = place_ref[number]
        inside = lax.rem(place, half_heads)
        rows = jnp.where(place < half_heads, kept_ref[inside], received_ref[inside])
        weights = jnp.concatenate(
            [weight_refs[2 * at][...], weight_refs[2 * at + 1][...]], axis=0
        )
        product = jnp.dot(rows, weights, preferred_element_type=jnp.float32)
        total = product if total is None else total + product
    for place, out_ref in enumerate(out_refs):
        piece = total[place * tokens : (place + 1) * tokens]
        out_ref[...] = piece + start_refs[place][...] if carried else piece


def project(places, numbers, kept, received, starts, weights):
    shape = (kept.shape[1] // 2, weights[0].shape[1])
    arrays = [kept, received, *starts, *weights]
    return pl.pallas_call(
        functools.partial(project_kernel, numbers, bool(starts)),
        grid_spec=pltpu.PrefetchScalarGridSpec(
            num_scalar_prefetch=1,
            grid=(1,),
            in_specs=[whole(array.shape) for array in arrays],
            out_specs=[whole(shape)] * 2,
        ),
        out_shape=[jax.ShapeDtypeStruct(shape, jnp.float32)] * 2,
        compiler_params=pltpu.CompilerParams(vmem_limit_bytes=16 << 20),
    )(places, *arrays)


def norm_kernel(residual_ref, mine_ref, theirs_ref, gain_ref, share_ref, mixture_ref, sent_ref):
    mixture = residual_ref[...].astype(jnp.float32) + mine_ref[...] + theirs_ref[...]
    mixture_ref[...] = mixture
    mean = jnp.mean(mixture * mixture, axis=-1, keepdims=True)
    normed = (mixture * lax.rsqrt(mean + 1e-06) * gain_ref[...]).astype(jnp.bfloat16)
    sent_ref[...] = jnp.concatenate([normed, share_ref[...]], axis=1)


def expert_kernel(count, *refs):
    row_refs, chooser_ref, weight_refs, out_refs = (
        refs[:count],
        refs[count],
        refs[count + 1 : count + 7],
        refs[count + 7 :],
    )
    width = 2 * out_refs[0].shape[1]
    rows = jnp.concatenate([row_ref[:, :width] for row_ref in row_refs], axis=0)
    parts = jnp.concatenate([row_ref[:, width:] for row_ref in row_refs], axis=0)
    shares = jnp.dot(parts, chooser_ref[...], preferred_element_type=jnp.float32)
    hidden = weight_refs[0].shape[1]
    tile = 256 if hidden % 256 == 0 else hidden
    result = None
    for number in range(2):
        gate_ref, up_ref, down_ref = weight_refs[3 * number : 3 * number + 3]
        answer = None
        for begin in range(0, hidden, tile):
            inside = slice(begin, begin + tile)
            gate = jnp.dot(rows, gate_ref[:, inside], preferred_element_type=jnp.float32)
            upper = jnp.dot(rows, up_ref[:, inside], preferred_element_type=jnp.float32)
            middle = (gate / (1.0 + jnp.exp(-gate)) * upper).astype(jnp.bfloat16)
            piece = jnp.dot(middle, down_ref[inside, :], preferred_element_type=jnp.float32)
            answer = piece if answer is None else answer + piece
        rounded = answer.astype(jnp.bfloat16).astype(jnp.float32)
        weighted = rounded * shares[:, number : number + 1]
        result = weighted if result is None else result + weighted
    begin = 0
    for left_ref, right_ref in zip(out_refs[0::2], out_refs[1::2]):
        piece = result[begin : begin + left_ref.shape[0]]
        begin += left_ref.shape[0]
        left_ref[...] = piece[:, : width // 2].astype(left_ref.dtype)
        right_ref[...] = piece[:, width // 2 :].astype(right_ref.dtype)


def load_kernel(*refs):
    count = len(refs) // 2
    copies = [
        pltpu.make_async_copy(refs[n], refs[count + n], refs[2 * count].at[n])
        for n in range(count)
    ]
    for copy in copies:
        copy.start()
    for copy in copies:
        copy.wait()


def load(arrays):
    return pl.pallas_call(
        load_kernel,
        in_specs=[pl.BlockSpec(memory_space=pl.ANY)] * len(arrays),
        out_specs=[pl.BlockSpec(memory_space=pltpu.VMEM)] * len(arrays),
        out_shape=[jax.ShapeDtypeStruct(array.shape, array.dtype) for array in arrays],
        scratch_shapes=[pltpu.SemaphoreType.DMA((len(arrays),))],
        compiler_params=pltpu.CompilerParams(vmem_limit_bytes=24 << 20),
    )(*arrays)


def run_experts(pieces, chooser, experts, split):
    shape = (pieces[0].shape[0], experts[0][0].shape[0] // 2)
    results = [jax.ShapeDtypeStruct(shape, jnp.float32)] * (2 * len(pieces))
    if split:
        halved = (shape[0] // 2, shape[1])
        results[:2] = [jax.ShapeDtypeStruct(halved, jnp.bfloat16)] * 4
    arrays = [*pieces, chooser, *experts[0], *experts[1]]
    inside = pl.BlockSpec(memory_space=pltpu.VMEM)
    return pl.pallas_call(
        functools.partial(expert_kernel, len(pieces)),
        in_specs=[whole(array.shape) for array in arrays[:-6]] + [inside] * 6,
        out_specs=[whole(result.shape) for result in results],
        grid=(1,),
        out_shape=results,
        compiler_params=pltpu.CompilerParams(vmem_limit_bytes=16 << 20),
    )(*arrays)


def ring_body(
    residual_in,
    queries,
    question_key_values,
    document_prefix_cache,
    out_proj,
    norm_gain,
    routes,
    keep_mask,
    route_weights,
    expert_slots,
    expert_gate,
    expert_up,
    expert_down,
):
    local_tokens = queries.shape[0]
    line = lax.axis_index("line")
    lines = lax.axis_size("line")
    pairs = lines // 2
    last = pairs // 2
    member = line & 1
    other = 1 - member
    offsets = list(range(-last, pairs - last))

    table = []
    for device in range(lines):
        spot = ring_spot(device // 2, pairs)
        held = [ring_pair((spot + offset) % pairs, pairs) for offset in offsets]
        table.append([(pair // last ^ device % 2) * last + pair % last for pair in held])
    places = lax.dynamic_index_in_dim(jnp.array(table, jnp.int32), line, 0, keepdims=False)

    def half(array, which):
        return lax.dynamic_slice_in_dim(
            array, which * (array.shape[1] // 2), array.shape[1] // 2, axis=1
        )

    def both(left, right, which):
        return jnp.concatenate([half(left, which), half(right, which)], axis=1)

    arrived = ring_gather(document_prefix_cache)
    prefix = []
    for offset in offsets:
        prefix += [arrived[offset], swap(arrived[offset])]
    cut = out_proj.shape[0] // 2
    upper_rows = ring_gather(out_proj[:cut])
    lower_rows = ring_gather(out_proj[cut:], True)
    lower_rows[-1], queries, question_key_values, routes, keep_mask, route_weights = (
        lax.optimization_barrier(
            (lower_rows[-1], queries, question_key_values, routes, keep_mask, route_weights)
        )
    )

    slots = expert_slots.shape[0]
    lanes = -(-3 * slots // HEAD_SIZE) * HEAD_SIZE
    pieces = three_parts(slot_weights(routes, keep_mask, route_weights, expert_slots))
    pieces.append(jnp.zeros((local_tokens, lanes - 3 * slots), jnp.bfloat16))
    slot_parts = jnp.concatenate(pieces, axis=1)
    lane = np.arange(lanes)
    slot_of_lane = jnp.array(np.where(lane < 3 * slots, lane % slots, -1), jnp.int32)
    wanted = jnp.stack([line, line ^ 1])
    chooser = (slot_of_lane[:, None] == wanted[None, :]).astype(jnp.bfloat16)

    mine = (expert_gate[0], expert_up[0], expert_down[0])
    experts = (mine, tuple(swap(array) for array in mine))

    kv_columns = KEY_VALUE_HEADS * HEAD_SIZE
    question_keys = question_key_values[:, :kv_columns]
    question_values = question_key_values[:, kv_columns:]
    own_pack = jnp.concatenate(
        [half(queries, member), both(question_keys, question_values, member)], axis=1
    )
    send_pack = jnp.concatenate(
        [half(queries, other), both(question_keys, question_values, other)], axis=1
    )
    own_pack, send_pack, places, slot_parts, chooser = lax.optimization_barrier(
        (own_pack, send_pack, places, slot_parts, chooser)
    )
    kept, sent = attention(member, own_pack, swap(send_pack), prefix)

    early = [o for o in offsets if abs(o) < last - 1]
    late = [o for o in offsets if abs(o) >= last - 1]
    batches = [[0, -1, 1]] + [[-step, step] for step in range(2, last)] + [[-last]]
    received = swap(sent)
    received, theirs = lax.optimization_barrier((received, experts[1]))

    def projected(batch, starts):
        numbers = tuple(offsets.index(o) for o in batch)
        return project(
            places,
            numbers,
            kept,
            received,
            starts,
            [array[o] for o in batch for array in (upper_rows, lower_rows)],
        )

    for_me, for_partner = projected(late, projected(early, []))
    shape = residual_in.shape
    mixture, normed = pl.pallas_call(
        norm_kernel,
        out_shape=[
            jax.ShapeDtypeStruct(shape, jnp.float32),
            jax.ShapeDtypeStruct((shape[0], shape[1] + lanes), jnp.bfloat16),
        ],
        compiler_params=pltpu.CompilerParams(vmem_limit_bytes=8 << 20),
    )(residual_in, for_me, swap(for_partner), norm_gain[None, :], slot_parts)

    rows = ring_gather(normed)
    held = load([*mine, *theirs])
    experts = (held[:3], held[3:])
    left, right = {}, {}
    for batch in batches:
        found = run_experts([rows[o] for o in batch], chooser, experts, batch == [-last])
        for parts, pieces in ((left, found[0::2]), (right, found[1::2])):
            if batch == [-last]:
                parts[-last] = tuple(pieces)
            else:
                parts.update(zip(batch, pieces))
    expert_sum = jnp.concatenate([ring_sum(left), ring_sum(right)], axis=1)
    return (mixture + expert_sum).astype(jnp.bfloat16)


def solution(mesh):
    placed = (
        P(("group", "line"), None),
        P(("group", "line"), None),
        P(("group", "line"), None),
        P(("group", "line"), None),
        P("line", None),
        P(),
        P(("group", "line"), None),
        P(("group", "line"), None),
        P(("group", "line"), None),
        P(),
        P("line", None, None),
        P("line", None, None),
        P("line", None, None),
    )

    tokens_of = lambda arrays: arrays[1].shape[0] // mesh.size

    def layer(*arrays):
        tokens, experts = tokens_of(arrays), arrays[9].shape[0]
        dense = 2 * (tokens * TOPK // experts) >= tokens
        ring = dense and mesh.shape["line"] == QUERY_HEADS and experts == mesh.shape["line"]
        return jax.shard_map(
            ring_body if ring else body,
            mesh=mesh,
            in_specs=placed,
            out_specs=P(("group", "line"), None),
            check_vma=False,
        )(*arrays)

    return layer
```

```python
import functools
import math

import jax
import jax.numpy as jnp
import numpy as np
from jax import lax
from jax.experimental import pallas as pl
from jax.experimental.pallas import tpu as pltpu
from jax.sharding import PartitionSpec as P


QUERY_HEADS = 16
KEY_VALUE_HEADS = 2
HEAD_SIZE = 128
TOPK = 8
QLEN = 16


def partner(array, axis, bit):
    return lax.ppermute(array, axis, [(i, i ^ 1 << bit) for i in range(lax.axis_size(axis))])


def shifted(value, axis, steps):
    count = lax.axis_size(axis)
    pairs = [(source, (source + steps) % count) for source in range(count)]
    return lax.ppermute(value, axis, pairs)


def expert_answers(received, expert_gate, expert_up, expert_down):
    buffer_shape = received.shape
    flat_rows = received.reshape(-1, buffer_shape[-1])
    gate_proj = jnp.dot(flat_rows, expert_gate[0], preferred_element_type=jnp.float32)
    upper = jnp.dot(flat_rows, expert_up[0], preferred_element_type=jnp.float32)
    middle = (jax.nn.silu(gate_proj) * upper).astype(jnp.bfloat16)
    return (
        jnp.dot(middle, expert_down[0], preferred_element_type=jnp.float32)
        .astype(jnp.bfloat16)
        .reshape(buffer_shape)
    )


def mix_experts(
    normed_rows,
    route_rows,
    keep_rows,
    weight_rows,
    expert_slots,
    expert_gate,
    expert_up,
    expert_down,
    slot_cap,
):
    row_count = normed_rows.shape[0]
    model_width = normed_rows.shape[1]
    line_count = lax.axis_size("line")
    pair_count = row_count * TOPK
    expert_ids = route_rows.reshape(pair_count)
    kept_pairs = keep_rows.reshape(pair_count) > 0
    numbers = jnp.arange(expert_slots.shape[0], dtype=jnp.int32)
    matches = expert_ids[:, None] == numbers[None, :]
    target = jnp.sum(jnp.where(matches, expert_slots[None, :], 0), axis=1)
    chosen = (matches & kept_pairs[:, None]).astype(jnp.bfloat16)
    pair_order = jnp.arange(pair_count, dtype=jnp.int32)
    earlier = (pair_order[:, None] > pair_order[None, :]).astype(jnp.bfloat16)
    before = jnp.dot(earlier, chosen, preferred_element_type=jnp.float32)
    slot_rank = jnp.sum(before * chosen.astype(jnp.float32), axis=1).astype(jnp.int32)
    slot_index = jnp.where(kept_pairs, target * slot_cap + slot_rank, line_count * slot_cap)
    slot_owner = (
        jnp.full((line_count * slot_cap,), pair_count, jnp.int32)
        .at[slot_index]
        .set(pair_order, mode="drop")
    )
    source_row = jnp.where(slot_owner < pair_count, slot_owner // TOPK, row_count)
    padded = jnp.concatenate([normed_rows, jnp.zeros((1, model_width), jnp.bfloat16)], axis=0)
    buffer = padded[source_row].reshape(line_count, slot_cap, model_width)
    returned = lax.all_to_all(
        expert_answers(
            lax.all_to_all(buffer, "line", split_axis=0, concat_axis=0, tiled=True),
            expert_gate,
            expert_up,
            expert_down,
        ),
        "line",
        split_axis=0,
        concat_axis=0,
        tiled=True,
    )
    padded_back = jnp.concatenate(
        [
            returned.reshape(line_count * slot_cap, model_width),
            jnp.zeros((1, model_width), jnp.bfloat16),
        ],
        axis=0,
    )
    per_pair = padded_back[slot_index].reshape(row_count, TOPK, model_width)
    weight = jnp.where(kept_pairs, weight_rows.reshape(pair_count), 0.0).reshape(row_count, TOPK)
    return jnp.sum(per_pair.astype(jnp.float32) * weight[:, :, None], axis=1)


def near_state(heads_of_queries, local_keys, local_values, score_scale):
    local_tokens = heads_of_queries.shape[0]
    near_scores = (
        jnp.einsum(
            "thgd,shd->thgs", heads_of_queries, local_keys, preferred_element_type=jnp.float32
        )
        * score_scale
    )
    position = jnp.arange(local_tokens, dtype=jnp.int32)
    visible_mask = (position[:, None] // QLEN == position[None, :] // QLEN) & (
        position[None, :] <= position[:, None]
    )
    near_scores = jnp.where(visible_mask[:, None, None, :], near_scores, -1e30)
    run_max = near_scores.max(-1)
    exp_terms = jnp.exp(near_scores - run_max[..., None])
    run_sum = exp_terms.sum(-1)
    run_acc = jnp.einsum(
        "thgs,shd->thgd",
        exp_terms.astype(jnp.bfloat16),
        local_values,
        preferred_element_type=jnp.float32,
    )
    return (run_max, run_sum, run_acc)


def fold_block(carry, piece, heads_of_queries, kv_heads, score_scale):
    old_max, old_sum, old_acc = carry
    piece_rows = piece.shape[0]
    piece_keys = piece[:, : kv_heads * HEAD_SIZE].reshape(piece_rows, kv_heads, HEAD_SIZE)
    piece_vals = piece[:, kv_heads * HEAD_SIZE :].reshape(piece_rows, kv_heads, HEAD_SIZE)
    far_scores = (
        jnp.einsum(
            "thgd,nhd->thgn", heads_of_queries, piece_keys, preferred_element_type=jnp.float32
        )
        * score_scale
    )
    new_max = jnp.maximum(old_max, far_scores.max(-1))
    factor = jnp.exp(old_max - new_max)
    far_terms = jnp.exp(far_scores - new_max[..., None])
    new_acc = old_acc * factor[..., None] + jnp.einsum(
        "thgn,nhd->thgd",
        far_terms.astype(jnp.bfloat16),
        piece_vals,
        preferred_element_type=jnp.float32,
    )
    return (new_max, old_sum * factor + far_terms.sum(-1), new_acc)


def body(
    residual_in,
    queries,
    question_key_values,
    document_prefix_cache,
    out_proj,
    norm_gain,
    routes,
    keep_mask,
    route_weights,
    expert_slots,
    expert_gate,
    expert_up,
    expert_down,
):
    local_tokens = queries.shape[0]
    queries_per_key_head = QUERY_HEADS // KEY_VALUE_HEADS
    score_scale = 1.0 / math.sqrt(HEAD_SIZE)
    half_kv = KEY_VALUE_HEADS // 2
    query_width = half_kv * queries_per_key_head * HEAD_SIZE
    kv_width = half_kv * HEAD_SIZE
    member = lax.axis_index("line") % 2
    other = 1 - member
    query_split = queries.reshape(local_tokens, 2, query_width)
    key_split = question_key_values[:, : KEY_VALUE_HEADS * HEAD_SIZE].reshape(
        local_tokens, 2, kv_width
    )
    value_split = question_key_values[:, KEY_VALUE_HEADS * HEAD_SIZE :].reshape(
        local_tokens, 2, kv_width
    )
    own_pack = jnp.concatenate(
        [
            lax.dynamic_index_in_dim(query_split, member, 1, keepdims=False),
            lax.dynamic_index_in_dim(key_split, member, 1, keepdims=False),
            lax.dynamic_index_in_dim(value_split, member, 1, keepdims=False),
        ],
        axis=1,
    )
    send_pack = jnp.concatenate(
        [
            lax.dynamic_index_in_dim(query_split, other, 1, keepdims=False),
            lax.dynamic_index_in_dim(key_split, other, 1, keepdims=False),
            lax.dynamic_index_in_dim(value_split, other, 1, keepdims=False),
        ],
        axis=1,
    )
    partner_pack = partner(send_pack, "line", 0)
    both_pack = jnp.concatenate([own_pack, partner_pack], axis=0)
    pair_rows = both_pack.shape[0]
    heads_of_queries = both_pack[:, :query_width].reshape(
        pair_rows, half_kv, queries_per_key_head, HEAD_SIZE
    )
    local_keys = both_pack[:, query_width : query_width + kv_width].reshape(
        pair_rows, half_kv, HEAD_SIZE
    )
    local_values = both_pack[:, query_width + kv_width :].reshape(pair_rows, half_kv, HEAD_SIZE)
    start_state = near_state(heads_of_queries, local_keys, local_values, score_scale)
    prefix_rows = document_prefix_cache.shape[0]
    document_keys = document_prefix_cache[:, : KEY_VALUE_HEADS * HEAD_SIZE].reshape(
        prefix_rows, 2, kv_width
    )
    document_values = document_prefix_cache[:, KEY_VALUE_HEADS * HEAD_SIZE :].reshape(
        prefix_rows, 2, kv_width
    )
    own_slab = jnp.concatenate(
        [
            lax.dynamic_index_in_dim(document_keys, member, 1, keepdims=False),
            lax.dynamic_index_in_dim(document_values, member, 1, keepdims=False),
        ],
        axis=1,
    )
    send_slab = jnp.concatenate(
        [
            lax.dynamic_index_in_dim(document_keys, other, 1, keepdims=False),
            lax.dynamic_index_in_dim(document_values, other, 1, keepdims=False),
        ],
        axis=1,
    )
    slab = jnp.concatenate([own_slab, partner(send_slab, "line", 0)], axis=0)
    levels = (lax.axis_size("line") // 2).bit_length() - 1
    for level in range(levels):
        slab = jnp.concatenate([slab, shifted(slab, "line", 2 * (1 << level))], axis=0)
    slab_rows = slab.shape[0]
    block_rows = math.gcd(slab_rows, 2048)
    slab_blocks = slab.reshape(slab_rows // block_rows, block_rows, 2 * kv_width)

    def scan_step(carry, piece):
        return (fold_block(carry, piece, heads_of_queries, half_kv, score_scale), None)

    final_state, _ = lax.scan(scan_step, start_state, slab_blocks)
    _, run_sum, run_acc = final_state
    pair_context = (
        (run_acc / run_sum[..., None]).reshape(pair_rows, query_width).astype(jnp.bfloat16)
    )
    mine = pair_context[:local_tokens]
    returned_context = partner(pair_context[local_tokens:], "line", 0)
    context_rows = jnp.where(
        member == 0,
        jnp.concatenate([mine, returned_context], axis=1),
        jnp.concatenate([returned_context, mine], axis=1),
    )
    attended = jnp.dot(
        context_rows,
        lax.all_gather(out_proj, "line", axis=0, tiled=True),
        preferred_element_type=jnp.float32,
    )
    mixture = residual_in.astype(jnp.float32) + attended
    normed = (
        mixture * lax.rsqrt(jnp.mean(mixture * mixture, axis=-1, keepdims=True) + 1e-06) * norm_gain
    ).astype(jnp.bfloat16)
    half_cap = local_tokens * TOPK // expert_slots.shape[0]
    expert_sum = mix_experts(
        normed,
        routes,
        keep_mask,
        route_weights,
        expert_slots,
        expert_gate,
        expert_up,
        expert_down,
        2 * half_cap,
    )
    return (mixture + expert_sum).astype(jnp.bfloat16)


def ring_spot(pair, pairs):
    row, column = divmod(pair, 2)
    return row if column == 0 else pairs - 1 - row


def ring_pair(spot, pairs):
    return 2 * spot if spot < pairs // 2 else 2 * (pairs - 1 - spot) + 1


def around(value, steps):
    count = lax.axis_size("line")
    pairs = count // 2
    moves = [
        (i, 2 * ring_pair((ring_spot(i // 2, pairs) + steps) % pairs, pairs) + i % 2)
        for i in range(count)
    ]
    return lax.ppermute(value, "line", moves)


def swap(value):
    return partner(value, "line", 0)


def ring_gather(value, last_back=False):
    last = lax.axis_size("line") // 4
    found = {0: value}
    for step in range(1, last):
        found[-step] = around(found[1 - step], 1)
        found[step] = around(found[step - 1], -1)
    if last_back:
        found[-last] = around(found[last - 1], -1)
    else:
        found[-last] = around(found[1 - last], 1)
    return found


def ring_sum(parts):
    pairs = len(parts)
    last = pairs // 2
    first_half, second_half = parts[-last]
    cut = first_half.shape[0]
    forward = around(first_half.astype(jnp.bfloat16), 1).astype(jnp.float32)
    backward = around(second_half.astype(jnp.bfloat16), -1).astype(jnp.float32)
    for step in range(2, last + 1):
        ahead = parts[last + 1 - step]
        behind = parts[step - last - 1]
        if step == 2:
            forward = jnp.concatenate([ahead[:cut] + forward, ahead[cut:]], axis=0)
            backward = jnp.concatenate([behind[:cut], behind[cut:] + backward], axis=0)
        else:
            forward = ahead + forward
            backward = behind + backward
        forward = around(forward.astype(jnp.bfloat16), 1).astype(jnp.float32)
        backward = around(backward.astype(jnp.bfloat16), -1).astype(jnp.float32)
    return parts[0] + forward + backward


def slot_weights(route_rows, keep_rows, weight_rows, expert_slots):
    numbers = jnp.arange(expert_slots.shape[0], dtype=jnp.int32)
    target = jnp.sum(
        jnp.where(route_rows[:, :, None] == numbers, expert_slots[None, None, :], 0), axis=2
    )
    kept = jnp.where(keep_rows > 0, weight_rows, 0.0)
    return jnp.sum(jnp.where(target[:, :, None] == numbers, kept[:, :, None], 0.0), axis=1)


def three_parts(values):
    high = lax.reduce_precision(values, 8, 7)
    rest = values - high
    middle = lax.reduce_precision(rest, 8, 7)
    return [part.astype(jnp.bfloat16) for part in (high, middle, rest - middle)]


def whole(shape):
    return pl.BlockSpec(shape, lambda *_: (0,) * len(shape))


def attention_kernel(begin, end, member_ref, *refs):
    own_ref, partner_ref = refs[:2]
    prefix_refs, (kept_ref, sent_ref, keys, values) = refs[2:-4], refs[-4:]
    if begin:
        prefix_refs, earlier = prefix_refs[:-2], prefix_refs[-2:]
        kept_ref[:begin] = earlier[0][...]
        sent_ref[:begin] = earlier[1][...]
    tokens = own_ref.shape[0]
    rows = 2 * tokens
    scale = 1.0 / math.sqrt(HEAD_SIZE)
    query_width = own_ref.shape[1] - 2 * HEAD_SIZE
    contract_last = (((1,), (1,)), ((), ()))

    held = prefix_refs[0].shape[0]
    key_at = pl.multiple_of(member_ref[0] * HEAD_SIZE, HEAD_SIZE)
    value_at = pl.multiple_of((KEY_VALUE_HEADS + member_ref[0]) * HEAD_SIZE, HEAD_SIZE)
    for number, prefix_ref in enumerate(prefix_refs):
        inside = slice(number * held, (number + 1) * held)
        keys[inside, :] = prefix_ref[:, pl.ds(key_at, HEAD_SIZE)]
        values[inside, :] = prefix_ref[:, pl.ds(value_at, HEAD_SIZE)]

    def columns(start):
        at = pl.ds(start, HEAD_SIZE)
        return jnp.concatenate([own_ref[:, at], partner_ref[:, at]], axis=0)

    near_keys = columns(query_width)
    near_values = columns(query_width + HEAD_SIZE)
    row = lax.rem(lax.broadcasted_iota(jnp.int32, (2 * rows, rows), 0), rows)
    column = lax.broadcasted_iota(jnp.int32, (2 * rows, rows), 1)
    visible = (lax.div(row, QLEN) == lax.div(column, QLEN)) & (column <= row)

    def two_heads(number, carry):
        start = pl.multiple_of(2 * number * HEAD_SIZE, 2 * HEAD_SIZE)
        query = jnp.concatenate([columns(start), columns(start + HEAD_SIZE)], axis=0)
        near = lax.dot_general(query, near_keys, contract_last, preferred_element_type=jnp.float32)
        near = jnp.where(visible, near * scale, -1e30)
        far = lax.dot_general(query, keys[...], contract_last, preferred_element_type=jnp.float32)
        far = far * scale
        largest = jnp.maximum(near.max(axis=1, keepdims=True), far.max(axis=1, keepdims=True))
        near_terms, far_terms = jnp.exp(near - largest), jnp.exp(far - largest)
        total = near_terms.sum(axis=1, keepdims=True) + far_terms.sum(axis=1, keepdims=True)
        summed = jnp.dot(
            far_terms.astype(jnp.bfloat16), values[...], preferred_element_type=jnp.float32
        ) + jnp.dot(
            near_terms.astype(jnp.bfloat16), near_values, preferred_element_type=jnp.float32
        )
        result = (summed / total).astype(jnp.bfloat16)
        even, odd = result[:rows], result[rows:]
        first = member_ref[0] == 0
        kept_ref[number] = jnp.where(first, even, odd)
        sent = jnp.where(first, odd, even)
        sent_ref[number] = jnp.concatenate([sent[tokens:], sent[:tokens]], axis=0)
        return carry

    lax.fori_loop(begin, end, two_heads, 0)


def attention(member, own_pack, partner_pack, prefix, begin, end, earlier):
    tokens, width = own_pack.shape
    half_heads = (width // HEAD_SIZE - 2) // 2
    end = half_heads if end is None else end
    shape = (end, 2 * tokens, HEAD_SIZE)
    arrays = [own_pack, partner_pack, *prefix, *earlier]
    return pl.pallas_call(
        functools.partial(attention_kernel, begin, end),
        grid_spec=pltpu.PrefetchScalarGridSpec(
            num_scalar_prefetch=1,
            grid=(1,),
            in_specs=[whole(array.shape) for array in arrays],
            out_specs=[whole(shape)] * 2,
            scratch_shapes=[pltpu.VMEM((len(prefix) * prefix[0].shape[0], HEAD_SIZE), jnp.bfloat16)]
            * 2,
        ),
        out_shape=[jax.ShapeDtypeStruct(shape, jnp.bfloat16)] * 2,
        compiler_params=pltpu.CompilerParams(vmem_limit_bytes=24 << 20),
    )(member[None], *arrays)


def project_kernel(numbers, carried, place_ref, kept_ref, received_ref, *refs):
    start_refs = refs[: 2 * carried]
    weight_refs = refs[2 * carried : -2]
    out_refs = refs[-2:]
    half_heads = kept_ref.shape[0]
    tokens = out_refs[0].shape[0]
    total = None
    for at, number in enumerate(numbers):
        place = place_ref[number]
        inside = lax.rem(place, half_heads)
        rows = jnp.where(place < half_heads, kept_ref[inside], received_ref[inside])
        weights = jnp.concatenate(
            [weight_refs[2 * at][...], weight_refs[2 * at + 1][...]], axis=0
        )
        product = jnp.dot(rows, weights, preferred_element_type=jnp.float32)
        total = product if total is None else total + product
    for place, out_ref in enumerate(out_refs):
        piece = total[place * tokens : (place + 1) * tokens]
        out_ref[...] = piece + start_refs[place][...] if carried else piece


def project(places, numbers, kept, received, starts, weights):
    shape = (kept.shape[1] // 2, weights[0].shape[1])
    arrays = [kept, received, *starts, *weights]
    return pl.pallas_call(
        functools.partial(project_kernel, numbers, bool(starts)),
        grid_spec=pltpu.PrefetchScalarGridSpec(
            num_scalar_prefetch=1,
            grid=(1,),
            in_specs=[whole(array.shape) for array in arrays],
            out_specs=[whole(shape)] * 2,
        ),
        out_shape=[jax.ShapeDtypeStruct(shape, jnp.float32)] * 2,
        compiler_params=pltpu.CompilerParams(vmem_limit_bytes=16 << 20),
    )(places, *arrays)


def norm_kernel(residual_ref, mine_ref, theirs_ref, gain_ref, share_ref, mixture_ref, sent_ref):
    mixture = residual_ref[...].astype(jnp.float32) + mine_ref[...] + theirs_ref[...]
    mixture_ref[...] = mixture
    mean = jnp.mean(mixture * mixture, axis=-1, keepdims=True)
    normed = (mixture * lax.rsqrt(mean + 1e-06) * gain_ref[...]).astype(jnp.bfloat16)
    sent_ref[...] = jnp.concatenate([normed, share_ref[...]], axis=1)


def expert_kernel(count, *refs):
    row_refs, chooser_ref, weight_refs, out_refs = (
        refs[:count],
        refs[count],
        refs[count + 1 : count + 7],
        refs[count + 7 :],
    )
    width = 2 * out_refs[0].shape[1]
    rows = jnp.concatenate([row_ref[:, :width] for row_ref in row_refs], axis=0)
    parts = jnp.concatenate([row_ref[:, width:] for row_ref in row_refs], axis=0)
    shares = jnp.dot(parts, chooser_ref[...], preferred_element_type=jnp.float32)
    hidden = weight_refs[0].shape[1]
    tile = 256 if hidden % 256 == 0 else hidden
    result = None
    for number in range(2):
        gate_ref, up_ref, down_ref = weight_refs[3 * number : 3 * number + 3]
        answer = None
        for begin in range(0, hidden, tile):
            inside = slice(begin, begin + tile)
            gate = jnp.dot(rows, gate_ref[:, inside], preferred_element_type=jnp.float32)
            upper = jnp.dot(rows, up_ref[:, inside], preferred_element_type=jnp.float32)
            middle = (gate / (1.0 + jnp.exp(-gate)) * upper).astype(jnp.bfloat16)
            piece = jnp.dot(middle, down_ref[inside, :], preferred_element_type=jnp.float32)
            answer = piece if answer is None else answer + piece
        rounded = answer.astype(jnp.bfloat16).astype(jnp.float32)
        weighted = rounded * shares[:, number : number + 1]
        result = weighted if result is None else result + weighted
    begin = 0
    for left_ref, right_ref in zip(out_refs[0::2], out_refs[1::2]):
        piece = result[begin : begin + left_ref.shape[0]]
        begin += left_ref.shape[0]
        left_ref[...] = piece[:, : width // 2].astype(left_ref.dtype)
        right_ref[...] = piece[:, width // 2 :].astype(right_ref.dtype)


def load_kernel(*refs):
    count = len(refs) // 2
    copies = [
        pltpu.make_async_copy(refs[n], refs[count + n], refs[2 * count].at[n])
        for n in range(count)
    ]
    for copy in copies:
        copy.start()
    for copy in copies:
        copy.wait()


def load(arrays):
    return pl.pallas_call(
        load_kernel,
        in_specs=[pl.BlockSpec(memory_space=pl.ANY)] * len(arrays),
        out_specs=[pl.BlockSpec(memory_space=pltpu.VMEM)] * len(arrays),
        out_shape=[jax.ShapeDtypeStruct(array.shape, array.dtype) for array in arrays],
        scratch_shapes=[pltpu.SemaphoreType.DMA((len(arrays),))],
        compiler_params=pltpu.CompilerParams(vmem_limit_bytes=24 << 20),
    )(*arrays)


def run_experts(pieces, chooser, experts, split):
    shape = (pieces[0].shape[0], experts[0][0].shape[0] // 2)
    results = [jax.ShapeDtypeStruct(shape, jnp.float32)] * (2 * len(pieces))
    if split:
        halved = (shape[0] // 2, shape[1])
        results[:2] = [jax.ShapeDtypeStruct(halved, jnp.bfloat16)] * 4
    arrays = [*pieces, chooser, *experts[0], *experts[1]]
    inside = pl.BlockSpec(memory_space=pltpu.VMEM)
    return pl.pallas_call(
        functools.partial(expert_kernel, len(pieces)),
        in_specs=[whole(array.shape) for array in arrays[:-6]] + [inside] * 6,
        out_specs=[whole(result.shape) for result in results],
        grid=(1,),
        out_shape=results,
        compiler_params=pltpu.CompilerParams(vmem_limit_bytes=16 << 20),
    )(*arrays)


def ring_body(
    residual_in,
    queries,
    question_key_values,
    document_prefix_cache,
    out_proj,
    norm_gain,
    routes,
    keep_mask,
    route_weights,
    expert_slots,
    expert_gate,
    expert_up,
    expert_down,
):
    local_tokens = queries.shape[0]
    line = lax.axis_index("line")
    lines = lax.axis_size("line")
    pairs = lines // 2
    last = pairs // 2
    member = line & 1
    other = 1 - member
    offsets = list(range(-last, pairs - last))

    table = []
    for device in range(lines):
        spot = ring_spot(device // 2, pairs)
        held = [ring_pair((spot + offset) % pairs, pairs) for offset in offsets]
        table.append([(pair // last ^ device % 2) * last + pair % last for pair in held])
    places = lax.dynamic_index_in_dim(jnp.array(table, jnp.int32), line, 0, keepdims=False)

    def half(array, which):
        return lax.dynamic_slice_in_dim(
            array, which * (array.shape[1] // 2), array.shape[1] // 2, axis=1
        )

    def both(left, right, which):
        return jnp.concatenate([half(left, which), half(right, which)], axis=1)

    arrived = ring_gather(document_prefix_cache)
    prefix = []
    for offset in offsets:
        prefix += [arrived[offset], swap(arrived[offset])]
    cut = out_proj.shape[0] // 2
    upper_rows = ring_gather(out_proj[:cut])
    lower_rows = ring_gather(out_proj[cut:], True)
    lower_rows[-1], queries, question_key_values, routes, keep_mask, route_weights = (
        lax.optimization_barrier(
            (lower_rows[-1], queries, question_key_values, routes, keep_mask, route_weights)
        )
    )

    slots = expert_slots.shape[0]
    lanes = -(-3 * slots // HEAD_SIZE) * HEAD_SIZE
    pieces = three_parts(slot_weights(routes, keep_mask, route_weights, expert_slots))
    pieces.append(jnp.zeros((local_tokens, lanes - 3 * slots), jnp.bfloat16))
    slot_parts = jnp.concatenate(pieces, axis=1)
    lane = np.arange(lanes)
    slot_of_lane = jnp.array(np.where(lane < 3 * slots, lane % slots, -1), jnp.int32)
    wanted = jnp.stack([line, line ^ 1])
    chooser = (slot_of_lane[:, None] == wanted[None, :]).astype(jnp.bfloat16)

    mine = (expert_gate[0], expert_up[0], expert_down[0])
    experts = (mine, tuple(swap(array) for array in mine))

    kv_columns = KEY_VALUE_HEADS * HEAD_SIZE
    question_keys = question_key_values[:, :kv_columns]
    question_values = question_key_values[:, kv_columns:]
    own_pack = jnp.concatenate(
        [half(queries, member), both(question_keys, question_values, member)], axis=1
    )
    send_pack = jnp.concatenate(
        [half(queries, other), both(question_keys, question_values, other)], axis=1
    )
    own_pack, send_pack, places, slot_parts, chooser = lax.optimization_barrier(
        (own_pack, send_pack, places, slot_parts, chooser)
    )
    partner_pack = swap(send_pack)
    middle = QUERY_HEADS // KEY_VALUE_HEADS // 4
    earlier = attention(member, own_pack, partner_pack, prefix, 0, middle, [])
    kept, sent = attention(member, own_pack, partner_pack, prefix, middle, None, earlier)

    early = [o for o in offsets if abs(o) < last - 1]
    late = [o for o in offsets if abs(o) >= last - 1]
    batches = [[0, -1, 1]] + [[-step, step] for step in range(2, last)] + [[-last]]
    received = swap(sent)
    received, theirs = lax.optimization_barrier((received, experts[1]))

    def projected(batch, starts):
        numbers = tuple(offsets.index(o) for o in batch)
        return project(
            places,
            numbers,
            kept,
            received,
            starts,
            [array[o] for o in batch for array in (upper_rows, lower_rows)],
        )

    for_me, for_partner = projected(late, projected(early, []))
    shape = residual_in.shape
    mixture, normed = pl.pallas_call(
        norm_kernel,
        out_shape=[
            jax.ShapeDtypeStruct(shape, jnp.float32),
            jax.ShapeDtypeStruct((shape[0], shape[1] + lanes), jnp.bfloat16),
        ],
        compiler_params=pltpu.CompilerParams(vmem_limit_bytes=8 << 20),
    )(residual_in, for_me, swap(for_partner), norm_gain[None, :], slot_parts)

    rows = ring_gather(normed)
    held = load([*mine, *theirs])
    experts = (held[:3], held[3:])
    left, right = {}, {}
    for batch in batches:
        found = run_experts([rows[o] for o in batch], chooser, experts, batch == [-last])
        for parts, pieces in ((left, found[0::2]), (right, found[1::2])):
            if batch == [-last]:
                parts[-last] = tuple(pieces)
            else:
                parts.update(zip(batch, pieces))
    expert_sum = jnp.concatenate([ring_sum(left), ring_sum(right)], axis=1)
    return (mixture + expert_sum).astype(jnp.bfloat16)


def solution(mesh):
    placed = (
        P(("group", "line"), None),
        P(("group", "line"), None),
        P(("group", "line"), None),
        P(("group", "line"), None),
        P("line", None),
        P(),
        P(("group", "line"), None),
        P(("group", "line"), None),
        P(("group", "line"), None),
        P(),
        P("line", None, None),
        P("line", None, None),
        P("line", None, None),
    )

    tokens_of = lambda arrays: arrays[1].shape[0] // mesh.size

    def layer(*arrays):
        tokens, experts = tokens_of(arrays), arrays[9].shape[0]
        dense = 2 * (tokens * TOPK // experts) >= tokens
        ring = dense and mesh.shape["line"] == QUERY_HEADS and experts == mesh.shape["line"]
        return jax.shard_map(
            ring_body if ring else body,
            mesh=mesh,
            in_specs=placed,
            out_specs=P(("group", "line"), None),
            check_vma=False,
        )(*arrays)

    return layer
```
